32 devices in a mesh: dp: 4 (over y, x), expert: 8 (over z, core).
Axes of the slice: x: 2, y: 2, z: 4, core: 2. Of those that a mesh axis runs over, the one named last changes fastest.
Arguments:
- tokens: bfloat16 [1024, 1024], P(('dp', 'expert')), may hold values from -6 to 6
- cotangent: bfloat16 [1024, 1024], P(('dp', 'expert')), may hold values from -3 to 3
- routes: int32 [1024, 8], P(('dp', 'expert')), may hold values from 0 to 7, as said below
- combine: bfloat16 [1024, 8], P(('dp', 'expert')), may hold values from 0.099609375 to 1
- hot_experts: int32 [4], replicated, may hold values from 0 to 3, as said below
- extra_slots: int32 [4], replicated, may hold values from 1 to 4, as said below
- w_gate: bfloat16 [8, 1024, 384], P('expert'), may hold values from -0.1875 to 0.1875
- w_up: bfloat16 [8, 1024, 384], P('expert'), may hold values from -0.1875 to 0.1875
- w_down: bfloat16 [8, 384, 1024], P('expert'), may hold values from -0.3125 to 0.3125
Outputs:
- token_grads: bfloat16 [1024, 1024], P(('dp', 'expert'))
- grad_gate: bfloat16 [8, 1024, 384], P('expert', 'dp')
- grad_up: bfloat16 [8, 1024, 384], P('expert', 'dp')
- grad_down: bfloat16 [8, 384, 1024], P('expert')
The draws below stay inside these ranges and needn't reach their ends.
Inputs may be any that keep to these rules, and one draw needn't show every extreme that they name: `routes`: each row names 8 different experts. `hot_experts`: 4 different experts, all below 4. `extra_slots`: one of the entries equals 4.
All inputs are finite; a program needn't handle non-finite values.
Results may differ from the reference program's by a relative error of at most 0.0064.
Values may be sent and summed in bfloat16 or wider, within the bound.
A program may use at most 64 MiB of HBM per device.

```python
import jax
import jax.numpy as jnp
from jax import lax

D = 1024
HID = 384
TOP = 8
HOT = 4
TOK_DEV = 32
SPECIALIST_COUNT = 8
TOKENS = 1024
CAP = 16
EXTRA = 4


def route_tables(key):
    base_key = jax.random.fold_in(key, 4242)
    subkeys = jax.random.split(base_key, 7)
    middle_list = 1 + jax.random.permutation(subkeys[0], SPECIALIST_COUNT // 2 - 2)[:HOT - 2]
    ends_list = jnp.array([SPECIALIST_COUNT // 2 - 1, 0], dtype=jnp.int32)
    joined_list = jnp.concatenate([ends_list, middle_list.astype(jnp.int32)])
    hot_list = jax.random.permutation(subkeys[6], joined_list).astype(jnp.int32)
    extra_list = jax.random.randint(subkeys[1], (HOT,), 1, EXTRA + 1, dtype=jnp.int32)
    full_slot = jax.random.randint(subkeys[2], (), 0, HOT, dtype=jnp.int32)
    hot_order = jnp.arange(HOT, dtype=jnp.int32)
    extra_list = jnp.where(hot_order == full_slot, EXTRA, extra_list).astype(jnp.int32)
    specialist_saturated = jnp.sum(jnp.where(hot_order == full_slot, hot_list, 0))
    block_count = TOKENS // TOK_DEV
    block_keys = jax.random.split(subkeys[3], block_count)

    def block_order(block_key):
        return jax.random.permutation(block_key, TOK_DEV)
    position = jax.vmap(block_order)(block_keys).reshape(-1)
    mandated_assignment_choice = position < CAP + EXTRA
    specialist_dimension = jnp.arange(SPECIALIST_COUNT, dtype=jnp.int32)
    enrolled_marker = jnp.any(specialist_dimension[None, :] == hot_list[:, None], axis=0)
    stochastic_tosses = jax.random.randint(subkeys[4], (TOKENS, SPECIALIST_COUNT), 0, 2, dtype=jnp.int32)
    stochastic_jitter = jax.random.randint(subkeys[5], (TOKENS, SPECIALIST_COUNT), 0, 65536, dtype=jnp.int32)
    logit_increment = jnp.where(enrolled_marker[None, :], stochastic_tosses, 0)
    logit_increment = logit_increment + jnp.where((specialist_dimension[None, :] == specialist_saturated) & mandated_assignment_choice[:, None], 2, 0)
    gating_logits = (stochastic_jitter + logit_increment * 65536) * SPECIALIST_COUNT + specialist_dimension[None, :]
    chosen = lax.top_k(gating_logits, TOP)[1].astype(jnp.int32)
    return (hot_list, extra_list, chosen)


def draw_routes(key, part):
    return route_tables(key)[2]


def draw_hot_experts(key, part):
    return route_tables(key)[0]


def draw_extra_slots(key, part):
    return route_tables(key)[1]


def level_of(own_key, shape, pieces, smallest, top_value):
    loudness = 1.0
    for dim, parts in pieces:
        draws = jax.random.uniform(jax.random.fold_in(jax.random.fold_in(own_key, 6), dim), (parts,), jnp.float32, smallest / len(pieces), top_value / len(pieces))
        loudness = loudness * jnp.repeat(jnp.exp(draws), shape[dim] // parts).reshape((-1,) + (1,) * (len(shape) - 1 - dim))
    return loudness


def bell_draw(own_key, shape, spread, reach, cuts=(), kind=jnp.bfloat16):
    values = jax.random.normal(own_key, shape, jnp.float32) * spread
    if len(cuts) > 0:
        values = level_of(own_key, shape, cuts, -0.22, 0.18) * values
    return jnp.clip(values, min=-reach, max=reach).astype(kind)


def setup_inputs(seed: int = 0) -> dict:
    splits = jax.random.split(jax.random.key(seed), 10)
    tokens = bell_draw(splits[0], (TOKENS, D), 1.0, 6.0, ((0, 32),))
    cotangent = bell_draw(splits[1], (TOKENS, D), 0.5, 3.0, ((0, 32),))
    routes = draw_routes(jax.random.fold_in(splits[9], 71), 0)
    combine = jnp.clip(0.099609375 + 0.9003906 * jax.random.uniform(splits[3], (TOKENS, TOP), jnp.float32) ** level_of(splits[3], (TOKENS, TOP), ((0, 32),), -0.2, 0.2), 0.099609375, 1.0).astype(jnp.bfloat16)
    hot_experts = draw_hot_experts(jax.random.fold_in(splits[9], 71), 0)
    extra_slots = draw_extra_slots(jax.random.fold_in(splits[9], 71), 0)
    w_gate = bell_draw(splits[6], (SPECIALIST_COUNT, D, HID), D ** -0.5, 0.1875, ((0, 8),))
    w_up = bell_draw(splits[7], (SPECIALIST_COUNT, D, HID), D ** -0.5, 0.1875, ((0, 8),))
    w_down = bell_draw(splits[8], (SPECIALIST_COUNT, HID, D), HID ** -0.5, 0.3125, ((0, 8),))
    return dict(tokens=tokens, cotangent=cotangent, routes=routes, combine=combine, hot_experts=hot_experts, extra_slots=extra_slots, w_gate=w_gate, w_up=w_up, w_down=w_down)


def expert_pass(weight_gate, weight_up, weight_down, row_tokens, row_cotan, row_weights):
    gate_pre = jnp.dot(row_tokens, weight_gate, preferred_element_type=jnp.float32)
    up_proj = jnp.dot(row_tokens, weight_up, preferred_element_type=jnp.float32)
    sigmoid_gate = jax.nn.sigmoid(gate_pre)
    gate_act = gate_pre * sigmoid_gate
    hidden = (gate_act * up_proj).astype(jnp.bfloat16)
    out_grad = (row_weights.astype(jnp.float32)[:, None] * row_cotan.astype(jnp.float32)).astype(jnp.bfloat16)
    grad_down = jnp.dot(hidden.T, out_grad, preferred_element_type=jnp.float32)
    hidden_grad = jnp.dot(out_grad, weight_down.T, preferred_element_type=jnp.float32)
    gate_grad = (hidden_grad * up_proj * sigmoid_gate * (1.0 + gate_pre * (1.0 - sigmoid_gate))).astype(jnp.bfloat16)
    up_grad = (hidden_grad * gate_act).astype(jnp.bfloat16)
    grad_gate = jnp.dot(row_tokens.T, gate_grad, preferred_element_type=jnp.float32)
    grad_up = jnp.dot(row_tokens.T, up_grad, preferred_element_type=jnp.float32)
    row_grads = jnp.dot(gate_grad, weight_gate.T, preferred_element_type=jnp.float32)
    row_grads = row_grads + jnp.dot(up_grad, weight_up.T, preferred_element_type=jnp.float32)
    return row_grads.astype(jnp.bfloat16), (grad_gate, grad_up, grad_down)


def reference(tokens, cotangent, routes, combine, hot_experts, extra_slots, w_gate, w_up, w_down):
    block_count = TOKENS // TOK_DEV
    assign_count = TOK_DEV * TOP
    expert_ids = routes.reshape(block_count, assign_count)
    assign_order = jnp.arange(assign_count, dtype=jnp.int32)

    def rank_block(block_ids):
        earlier = (block_ids[:, None] == block_ids[None, :]) & (assign_order[None, :] < assign_order[:, None])
        return jnp.sum(earlier.astype(jnp.int32), axis=1)

    slot_rank = lax.map(rank_block, expert_ids)
    hot_match = expert_ids[:, :, None] == hot_experts[None, None, :]
    slot_limit = CAP + jnp.sum(jnp.where(hot_match, extra_slots[None, None, :], 0), axis=2)
    is_kept = slot_rank < slot_limit
    block_index = jnp.broadcast_to(jnp.arange(block_count, dtype=jnp.int32)[:, None], (block_count, assign_count))
    global_index = block_index * assign_count + assign_order[None, :]
    base_expert = jnp.where(slot_rank < CAP, expert_ids, SPECIALIST_COUNT)
    base_table = jnp.full((SPECIALIST_COUNT, block_count, CAP), -1, jnp.int32)
    base_table = base_table.at[base_expert, block_index, jnp.minimum(slot_rank, CAP - 1)].set(global_index, mode="drop")
    spill_kept = is_kept & (slot_rank >= CAP)
    spill_expert = jnp.where(spill_kept, expert_ids, SPECIALIST_COUNT)
    spill_table = jnp.full((SPECIALIST_COUNT, block_count, EXTRA), -1, jnp.int32)
    spill_table = spill_table.at[spill_expert, block_index, jnp.clip(slot_rank - CAP, 0, EXTRA - 1)].set(global_index, mode="drop")
    enrolled_marker = jnp.any(jnp.arange(SPECIALIST_COUNT, dtype=jnp.int32)[:, None] == hot_experts[None, :], axis=1)
    combine_flat = combine.reshape(-1)

    def rows_pass(weight_gate, weight_up, weight_down, table, accum):
        flat_table = table.reshape(-1)
        valid = flat_table >= 0
        safe_index = jnp.where(valid, flat_table, 0)
        token_index = safe_index // TOP
        row_weights = jnp.where(valid, combine_flat[safe_index], jnp.zeros((), combine.dtype))
        row_grads, grad_terms = expert_pass(weight_gate, weight_up, weight_down, tokens[token_index], cotangent[token_index], row_weights)
        accum = accum.at[token_index].add(row_grads.astype(jnp.float32))
        return accum, grad_terms

    def per_expert(accum, expert):
        weight_gate = w_gate[expert]
        weight_up = w_up[expert]
        weight_down = w_down[expert]
        accum, base_terms = rows_pass(weight_gate, weight_up, weight_down, base_table[expert], accum)

        def with_spill(current):
            return rows_pass(weight_gate, weight_up, weight_down, spill_table[expert], current)

        def without_spill(current):
            empty_gate = jnp.zeros((D, HID), jnp.float32)
            return current, (empty_gate, empty_gate, jnp.zeros((HID, D), jnp.float32))

        accum, spill_terms = lax.cond(enrolled_marker[expert], with_spill, without_spill, accum)
        totals = (
            (base_terms[0] + spill_terms[0]).astype(jnp.bfloat16),
            (base_terms[1] + spill_terms[1]).astype(jnp.bfloat16),
            (base_terms[2] + spill_terms[2]).astype(jnp.bfloat16),
        )
        return accum, totals

    accum, stacked = lax.scan(per_expert, jnp.zeros((TOKENS, D), jnp.float32), jnp.arange(SPECIALIST_COUNT, dtype=jnp.int32))
    return accum.astype(jnp.bfloat16), stacked[0], stacked[1], stacked[2]
```

```python
import functools

import jax
import jax.numpy as jnp
from jax import lax
from jax.experimental import pallas as pl
from jax.experimental.pallas import tpu as pltpu
from jax.sharding import PartitionSpec as P


def forward_rows(weight_gate, weight_up, weight_down, row_tokens, row_cotan, row_weights):
    gate_pre = jnp.dot(row_tokens, weight_gate, preferred_element_type=jnp.float32)
    up_proj = jnp.dot(row_tokens, weight_up, preferred_element_type=jnp.float32)
    sigmoid_gate = jax.nn.sigmoid(gate_pre)
    gate_act = gate_pre * sigmoid_gate
    hidden = (gate_act * up_proj).astype(jnp.bfloat16)
    out_grad = (row_weights.astype(jnp.float32)[:, None] * row_cotan.astype(jnp.float32)).astype(
        jnp.bfloat16
    )
    hidden_grad = jnp.dot(out_grad, weight_down.T, preferred_element_type=jnp.float32)
    gate_grad = (
        hidden_grad * up_proj * sigmoid_gate * (1.0 + gate_pre * (1.0 - sigmoid_gate))
    ).astype(jnp.bfloat16)
    up_grad = (hidden_grad * gate_act).astype(jnp.bfloat16)
    row_grads = jnp.dot(gate_grad, weight_gate.T, preferred_element_type=jnp.float32)
    row_grads = row_grads + jnp.dot(up_grad, weight_up.T, preferred_element_type=jnp.float32)
    return (row_grads.astype(jnp.bfloat16), (row_tokens, gate_grad, up_grad, hidden, out_grad))


def weight_terms(pieces):
    row_tokens, gate_grad, up_grad, hidden, out_grad = pieces
    grad_gate = jnp.dot(row_tokens.T, gate_grad, preferred_element_type=jnp.float32)
    grad_up = jnp.dot(row_tokens.T, up_grad, preferred_element_type=jnp.float32)
    grad_down = jnp.dot(hidden.T, out_grad, preferred_element_type=jnp.float32)
    return (grad_gate, grad_up, grad_down)


def expert_pass(weight_gate, weight_up, weight_down, row_tokens, row_cotan, row_weights):
    row_grads, pieces = forward_rows(
        weight_gate, weight_up, weight_down, row_tokens, row_cotan, row_weights
    )
    return (row_grads, weight_terms(pieces))


def shards(tokens, cotangent, routes, combine, hot_experts, extra_slots, w_gate, w_up, w_down):
    expert_count = lax.axis_size("expert")
    token_count, features = tokens.shape
    route_count = routes.shape[1]
    capacity = max(2, min(token_count * route_count * 7 // (8 * expert_count), token_count // 2))
    spare_slots = 2 * max(1, capacity // 6)
    expert_ids = routes.reshape(-1)
    assign_count = expert_ids.shape[0]
    assign_order = jnp.arange(assign_count, dtype=jnp.int32)
    earlier = (expert_ids[:, None] == expert_ids[None, :]) & (
        assign_order[None, :] < assign_order[:, None]
    )
    slot_rank = jnp.sum(earlier.astype(jnp.int32), axis=1)
    hot_match = expert_ids[:, None] == hot_experts[None, :]
    slot_limit = capacity + jnp.sum(jnp.where(hot_match, extra_slots[None, :], 0), axis=1)
    is_kept = slot_rank < slot_limit
    slot_count = capacity + spare_slots
    total_slots = expert_count * slot_count
    flat_slot = jnp.where(is_kept, expert_ids * slot_count + slot_rank, total_slots)
    slot_ids = jnp.arange(total_slots, dtype=jnp.int32)
    assign_onehot = slot_ids[:, None] == flat_slot[None, :]
    token_onehot = jnp.any(
        assign_onehot.reshape(total_slots, token_count, route_count), axis=2
    ).astype(jnp.bfloat16)
    both_rows = jnp.concatenate([tokens, cotangent], axis=1)
    filled = jnp.dot(token_onehot, both_rows, preferred_element_type=jnp.float32).astype(
        jnp.bfloat16
    )
    token_send = filled[:, :features].reshape(expert_count, slot_count, features)
    cotan_send = filled[:, features:].reshape(expert_count, slot_count, features)
    weight_flat = jnp.sum(
        jnp.where(assign_onehot, combine.reshape(-1).astype(jnp.float32)[None, :], 0.0), axis=1
    )
    weight_send = weight_flat.astype(jnp.bfloat16).reshape(expert_count, slot_count)
    token_recv, cotan_recv, weight_recv = (
        lax.all_to_all(token_send, "expert", split_axis=0, concat_axis=0, tiled=True),
        lax.all_to_all(cotan_send, "expert", split_axis=0, concat_axis=0, tiled=True),
        lax.all_to_all(weight_send, "expert", split_axis=0, concat_axis=0, tiled=True),
    )
    own_weights = (w_gate[0], w_up[0], w_down[0])
    all_rows, grad_terms = expert_pass(
        own_weights[0],
        own_weights[1],
        own_weights[2],
        token_recv.reshape(-1, features),
        cotan_recv.reshape(-1, features),
        weight_recv.reshape(-1),
    )
    grad_rows = all_rows.reshape(expert_count, slot_count, features)
    returned_rows = lax.all_to_all(grad_rows, "expert", split_axis=0, concat_axis=0, tiled=True)
    token_grads = jnp.dot(
        token_onehot.T,
        returned_rows.reshape(total_slots, features),
        preferred_element_type=jnp.float32,
    ).astype(jnp.bfloat16)
    grad_gate, grad_up = (
        lax.psum_scatter(grad_terms[0][None], "dp", scatter_dimension=1, tiled=True),
        lax.psum_scatter(grad_terms[1][None], "dp", scatter_dimension=1, tiled=True),
    )
    grad_down = lax.psum(grad_terms[2][None], "dp")
    return (
        token_grads,
        grad_gate.astype(jnp.bfloat16),
        grad_up.astype(jnp.bfloat16),
        grad_down.astype(jnp.bfloat16),
    )


MESH = pl.DeviceIdType.MESH
LANES = 128
TILE = 16
NT = (((1,), (1,)), ((), ()))
TN = (((0,), (0,)), ((), ()))


def slots_of(token_count, route_count, expert_count):
    capacity = max(2, min(token_count * route_count * 7 // (8 * expert_count), token_count // 2))
    return capacity, 2 * max(1, capacity // 6)


def dense_fits(sizes, token_count, features, route_count, hidden_size):
    capacity, spare = slots_of(token_count, route_count, sizes["expert"])
    return (
        route_count == sizes["expert"]
        and sizes["dp"] == 4
        and sizes["expert"] % 2 == 0
        and token_count == 2 * TILE
        and capacity == TILE
        and spare * 2 == 8
        and features % (8 * LANES) == 0
        and hidden_size % LANES == 0
    )


def dense_kernel(
    experts,
    tok_ref,
    cot_ref,
    routes_ref,
    comb_ref,
    hot_ref,
    extra_ref,
    wg_hbm,
    wu_hbm,
    wd_hbm,
    tg_ref,
    gg_out,
    gu_out,
    gd_out,
    slab,
    wg,
    wu,
    wd,
    all_t,
    all_og,
    all_h,
    all_gg,
    all_ug,
    row_out,
    pair_in,
    pair_sum,
    z_in,
    w_sem,
    send_sem,
    recv_sem,
    pair_send,
    pair_recv,
    z_send,
    z_recv,
):
    levels = experts // 2
    features = tok_ref.shape[1]
    blocks = features // LANES
    half = blocks // 2
    spill_at = 2 * blocks
    weight_at = spill_at + half
    bf16, f32 = jnp.bfloat16, jnp.float32

    d = lax.axis_index("dp")
    e = lax.axis_index("expert")
    z, c = e // 2, e % 2
    dx = d + 1 - 2 * (d % 2)
    dy = (d + 2) % 4
    dd = 3 - d
    pc = 1 - c

    def to(dp, level, core):
        return (dp, level * 2 + core)

    def slab_id(dp, level, core):
        return dp * experts + level * 2 + core

    weight_copies = [
        pltpu.make_async_copy(h.at[0], v, w_sem.at[i])
        for i, (h, v) in enumerate(((wg_hbm, wg), (wu_hbm, wu), (wd_hbm, wd)))
    ]
    for copy in weight_copies:
        copy.start()

    barrier = pltpu.get_barrier_semaphore()
    for peer in (to(dx, z, c), to(dy, z, c), to(d, z, pc)):
        pl.semaphore_signal(barrier, inc=1, device_id=peer, device_id_type=MESH)
    for step in range(1, levels):
        pl.semaphore_signal(
            barrier, inc=1, device_id=to(d, (z + step) % levels, c), device_id_type=MESH
        )

    me = slab_id(d, z, c)
    lane = lax.broadcasted_iota(jnp.int32, (2 * TILE, LANES), 1)
    row = lax.broadcasted_iota(jnp.int32, (2 * TILE, LANES), 0)
    routes = routes_ref[...]
    comb = comb_ref[...].astype(f32)
    weights = jnp.zeros((2 * TILE, LANES), f32)
    for k in range(routes.shape[1]):
        weights = jnp.where(lane == routes[:, k : k + 1], comb[:, k : k + 1], weights)
    limit = jnp.full((2 * TILE, LANES), TILE, jnp.int32)
    for j in range(hot_ref.shape[0]):
        limit = limit + jnp.where(lane == hot_ref[j], extra_ref[j], 0)
    weights = jnp.where(row < limit, weights, 0.0).astype(bf16)
    slab[me, weight_at] = weights[:TILE]
    slab[me, weight_at + 1] = weights[TILE:]
    tok_tail = tok_ref[TILE:, :].astype(f32)[:8]
    cot_tail = cot_ref[TILE:, :].astype(f32)[:8]
    tail_row = lax.broadcasted_iota(jnp.int32, (8, features), 0)
    spill = jnp.where(tail_row < 4, tok_tail, pltpu.roll(cot_tail, 4, 0))
    for j in range(blocks):
        cols = slice(j * LANES, (j + 1) * LANES)
        slab[me, j] = tok_ref[:TILE, cols]
        slab[me, blocks + j] = cot_ref[:TILE, cols]
    for j in range(half):
        lo = spill[:, j * LANES : (j + 1) * LANES]
        hi = spill[:, (half + j) * LANES : (half + j + 1) * LANES]
        slab[me, spill_at + j] = jnp.concatenate([lo, hi], axis=0).astype(bf16)

    pl.semaphore_wait(barrier, 3 + levels - 1)

    def copy_of(s, way, peer):
        return pltpu.make_async_remote_copy(
            src_ref=slab.at[s],
            dst_ref=slab.at[s],
            send_sem=send_sem.at[way, s],
            recv_sem=recv_sem.at[s],
            device_id=peer,
            device_id_type=MESH,
        )

    def to_x(s):
        return copy_of(s, 0, to(dx, z, c))

    def to_y(s):
        return copy_of(s, 1, to(dy, z, c))

    def to_pair(s):
        return copy_of(s, 2, to(d, z, pc))

    def to_up(s):
        return copy_of(s, 3, to(d, z + 1, c))

    def to_down(s):
        return copy_of(s, 4, to(d, z - 1, c))

    def arrived(s):
        to_pair(s).wait_recv()

    @pl.when(z + 1 < levels)
    def _():
        to_up(me).start()

    @pl.when(z > 0)
    def _():
        to_down(me).start()

    to_x(me).start()
    to_y(me).start()
    to_pair(me).start()

    for dist in range(1, levels):

        @pl.when(z - dist >= 0)
        def _():
            s = slab_id(d, z - dist, c)
            arrived(s)

            @pl.when(z + 1 < levels)
            def _():
                to_up(s).start()

            to_x(s).start()
            to_y(s).start()
            to_pair(s).start()

        @pl.when(z + dist < levels)
        def _():
            s = slab_id(d, z + dist, c)
            arrived(s)

            @pl.when(z > 0)
            def _():
                to_down(s).start()

            to_x(s).start()
            to_y(s).start()
            to_pair(s).start()

    for level in range(levels):
        arrived(slab_id(d, level, pc))

    main_rows = experts * TILE
    group_rows = main_rows + experts * 8
    own_lane = lax.broadcasted_iota(jnp.int32, (group_rows, LANES), 1) == e

    def group(dp, at):
        rows = pl.ds(at, group_rows)
        part = pl.ds(dp * experts, experts)

        def main(j):
            return slab[part, j].reshape(main_rows, LANES)

        lo, hi = [], []
        for j in range(half):
            both = slab[part, spill_at + j].astype(f32)
            lo.append(both[:, :8].reshape(experts * 8, LANES))
            hi.append(both[:, 8:].reshape(experts * 8, LANES))
        tail = jnp.concatenate(lo + hi, axis=1)
        cot_rows = pltpu.roll(tail, experts * 8 - 4, 0)
        w_main = main(weight_at).astype(f32)
        w_tail = slab[part, weight_at + 1].astype(f32)[:, :8].reshape(experts * 8, LANES)
        w = jnp.sum(
            jnp.where(own_lane, jnp.concatenate([w_main, w_tail], axis=0), 0.0),
            axis=1,
            keepdims=True,
        )
        all_t[rows, :] = jnp.concatenate(
            [jnp.concatenate([main(j) for j in range(blocks)], axis=1), tail.astype(bf16)], axis=0
        )
        cot = jnp.concatenate(
            [
                jnp.concatenate([main(blocks + j) for j in range(blocks)], axis=1).astype(f32),
                cot_rows,
            ],
            axis=0,
        )
        all_og[rows, :] = (w * cot).astype(bf16)
        t = all_t[rows, :]
        gate_pre = jnp.dot(t, wg[...], preferred_element_type=f32)
        up_proj = jnp.dot(t, wu[...], preferred_element_type=f32)
        hidden_grad = lax.dot_general(all_og[rows, :], wd[...], NT, preferred_element_type=f32)
        sig = jax.nn.sigmoid(gate_pre)
        act = gate_pre * sig
        all_h[rows, :] = (act * up_proj).astype(bf16)
        all_gg[rows, :] = (hidden_grad * up_proj * sig * (1.0 + gate_pre * (1.0 - sig))).astype(
            bf16
        )
        all_ug[rows, :] = (hidden_grad * act).astype(bf16)

    for copy in weight_copies:
        copy.wait()
    group(d, 0)
    own = pl.ds(0, group_rows)
    rg = lax.dot_general(all_gg[own, :], wg[...], NT, preferred_element_type=f32)
    rg = rg + lax.dot_general(all_ug[own, :], wu[...], NT, preferred_element_type=f32)
    for j in range(blocks):
        row_out[:, j] = (
            rg[:main_rows, j * LANES : (j + 1) * LANES].reshape(experts, TILE, LANES).astype(bf16)
        )
    for j in range(half):
        lo = rg[main_rows:, j * LANES : (j + 1) * LANES].reshape(experts, 8, LANES)
        hi = rg[main_rows:, (half + j) * LANES : (half + j + 1) * LANES].reshape(experts, 8, LANES)
        row_out[:, blocks + j] = jnp.concatenate([lo, hi], axis=1).astype(bf16)

    def pair_copy(level):
        return pltpu.make_async_remote_copy(
            src_ref=row_out.at[level * 2 + pc],
            dst_ref=pair_in.at[level],
            send_sem=pair_send.at[level],
            recv_sem=pair_recv.at[level],
            device_id=to(d, z, pc),
            device_id_type=MESH,
        )

    for level in range(levels):
        pair_copy(level).start()

    for level in range(levels):
        s = slab_id(dx, level, c)
        arrived(s)
        if level % 2 == 0:
            to_y(s).start()
        to_pair(s).start()
        s = slab_id(dy, level, c)
        arrived(s)
        if level % 2 == 1:
            to_x(s).start()
        to_pair(s).start()

    for level in range(levels):
        pair_copy(level).wait_recv()
        pair_sum[level] = (
            row_out[level * 2 + c].astype(f32) + pair_in[level].astype(f32)
        ).astype(bf16)

    def z_copy(step):
        level = (z + step) % levels
        return pltpu.make_async_remote_copy(
            src_ref=pair_sum.at[level],
            dst_ref=z_in.at[step - 1],
            send_sem=z_send.at[step - 1],
            recv_sem=z_recv.at[step - 1],
            device_id=to(d, level, c),
            device_id_type=MESH,
        )

    for step in range(1, levels):
        z_copy(step).start()

    for level in range(levels):
        arrived(slab_id(dx, level, pc))
    group(dx, group_rows)
    for level in range(levels):
        s = slab_id(dd, level, c)
        arrived(s)
        to_pair(s).start()
    for level in range(levels):
        arrived(slab_id(dy, level, pc))
    group(dy, 2 * group_rows)
    for level in range(levels):
        arrived(slab_id(dd, level, pc))
    group(dd, 3 * group_rows)

    share = features // 4
    t_cols = all_t[:, pl.ds(pl.multiple_of(d * share, LANES), share)]
    gg_out[0] = lax.dot_general(t_cols, all_gg[...], TN, preferred_element_type=f32).astype(bf16)
    gu_out[0] = lax.dot_general(t_cols, all_ug[...], TN, preferred_element_type=f32).astype(bf16)
    gd_out[0] = lax.dot_general(all_h[...], all_og[...], TN, preferred_element_type=f32).astype(
        bf16
    )

    total = pair_sum[z].astype(f32)
    for step in range(1, levels):
        z_copy(step).wait_recv()
        total = total + z_in[step - 1].astype(f32)
    for j in range(blocks):
        tg_ref[:TILE, j * LANES : (j + 1) * LANES] = total[j].astype(bf16)
    blank = jnp.zeros((8, LANES), f32)
    for j in range(half):
        tile = total[blocks + j]
        tg_ref[TILE:, j * LANES : (j + 1) * LANES] = jnp.concatenate(
            [tile[:8], blank], axis=0
        ).astype(bf16)
        tg_ref[TILE:, (half + j) * LANES : (half + j + 1) * LANES] = jnp.concatenate(
            [tile[8:], blank], axis=0
        ).astype(bf16)

    for level in range(levels):
        s = slab_id(d, level, c)
        to_x(s).wait_send()
        to_y(s).wait_send()
        to_pair(s).wait_send()
        if level % 2 == 0:
            to_y(slab_id(dx, level, c)).wait_send()
        else:
            to_x(slab_id(dy, level, c)).wait_send()
        for dp in (dx, dy, dd):
            to_pair(slab_id(dp, level, c)).wait_send()
        pair_copy(level).wait_send()

        @pl.when((z >= level) & (z + 1 < levels))
        def _():
            to_up(s).wait_send()

        @pl.when((z <= level) & (z > 0))
        def _():
            to_down(s).wait_send()

    for step in range(1, levels):
        z_copy(step).wait_send()


def dense_shards(tokens, cotangent, routes, combine, hot_experts, extra_slots, w_gate, w_up, w_down):
    experts = lax.axis_size("expert")
    replicas = lax.axis_size("dp")
    token_count, features = tokens.shape
    hidden_size = w_gate.shape[2]
    blocks = features // LANES
    levels = experts // 2
    tiles = 2 * blocks + blocks // 2 + 2
    back = blocks + blocks // 2
    rows = replicas * experts * (TILE + 8)
    bf16 = jnp.bfloat16
    vmem = pl.BlockSpec(memory_space=pltpu.VMEM)
    smem = pl.BlockSpec(memory_space=pltpu.SMEM)
    hbm = pl.BlockSpec(memory_space=pl.ANY)
    dma = pltpu.SemaphoreType.DMA
    return pl.pallas_call(
        functools.partial(dense_kernel, experts),
        out_shape=(
            jax.ShapeDtypeStruct((token_count, features), bf16),
            jax.ShapeDtypeStruct((1, features // replicas, hidden_size), bf16),
            jax.ShapeDtypeStruct((1, features // replicas, hidden_size), bf16),
            jax.ShapeDtypeStruct((1, hidden_size, features), bf16),
        ),
        in_specs=[vmem, vmem, vmem, vmem, smem, smem, hbm, hbm, hbm],
        out_specs=(vmem, vmem, vmem, vmem),
        scratch_shapes=[
            pltpu.VMEM((replicas * experts, tiles, TILE, LANES), bf16),
            pltpu.VMEM((features, hidden_size), bf16),
            pltpu.VMEM((features, hidden_size), bf16),
            pltpu.VMEM((hidden_size, features), bf16),
            pltpu.VMEM((rows, features), bf16),
            pltpu.VMEM((rows, features), bf16),
            pltpu.VMEM((rows, hidden_size), bf16),
            pltpu.VMEM((rows, hidden_size), bf16),
            pltpu.VMEM((rows, hidden_size), bf16),
            pltpu.VMEM((experts, back, TILE, LANES), bf16),
            pltpu.VMEM((levels, back, TILE, LANES), bf16),
            pltpu.VMEM((levels, back, TILE, LANES), bf16),
            pltpu.VMEM((levels - 1, back, TILE, LANES), bf16),
            dma((3,)),
            dma((5, replicas * experts)),
            dma((replicas * experts,)),
            dma((levels,)),
            dma((levels,)),
            dma((levels - 1,)),
            dma((levels - 1,)),
        ],
        compiler_params=pltpu.CompilerParams(
            collective_id=0, has_side_effects=True, vmem_limit_bytes=48 * 1024 * 1024
        ),
    )(tokens, cotangent, routes, combine, hot_experts, extra_slots, w_gate, w_up, w_down)


def solution(mesh):
    in_specs = (
        P(("dp", "expert"), None),
        P(("dp", "expert"), None),
        P(("dp", "expert"), None),
        P(("dp", "expert"), None),
        P(),
        P(),
        P("expert", None, None),
        P("expert", None, None),
        P("expert", None, None),
    )
    out_specs = (
        P(("dp", "expert"), None),
        P("expert", "dp", None),
        P("expert", "dp", None),
        P("expert", None, None),
    )

    def body(*args):
        token_count, features = args[0].shape
        if dense_fits(dict(mesh.shape), token_count, features, args[2].shape[1], args[6].shape[2]):
            return dense_shards(*args)
        return shards(*args)

    return jax.shard_map(body, mesh=mesh, in_specs=in_specs, out_specs=out_specs, check_vma=False)
```

```python
import functools

import jax
import jax.numpy as jnp
from jax import lax
from jax.experimental import pallas as pl
from jax.experimental.pallas import tpu as pltpu
from jax.sharding import PartitionSpec as P


def forward_rows(weight_gate, weight_up, weight_down, row_tokens, row_cotan, row_weights):
    gate_pre = jnp.dot(row_tokens, weight_gate, preferred_element_type=jnp.float32)
    up_proj = jnp.dot(row_tokens, weight_up, preferred_element_type=jnp.float32)
    sigmoid_gate = jax.nn.sigmoid(gate_pre)
    gate_act = gate_pre * sigmoid_gate
    hidden = (gate_act * up_proj).astype(jnp.bfloat16)
    out_grad = (row_weights.astype(jnp.float32)[:, None] * row_cotan.astype(jnp.float32)).astype(
        jnp.bfloat16
    )
    hidden_grad = jnp.dot(out_grad, weight_down.T, preferred_element_type=jnp.float32)
    gate_grad = (
        hidden_grad * up_proj * sigmoid_gate * (1.0 + gate_pre * (1.0 - sigmoid_gate))
    ).astype(jnp.bfloat16)
    up_grad = (hidden_grad * gate_act).astype(jnp.bfloat16)
    row_grads = jnp.dot(gate_grad, weight_gate.T, preferred_element_type=jnp.float32)
    row_grads = row_grads + jnp.dot(up_grad, weight_up.T, preferred_element_type=jnp.float32)
    return (row_grads.astype(jnp.bfloat16), (row_tokens, gate_grad, up_grad, hidden, out_grad))


def weight_terms(pieces):
    row_tokens, gate_grad, up_grad, hidden, out_grad = pieces
    grad_gate = jnp.dot(row_tokens.T, gate_grad, preferred_element_type=jnp.float32)
    grad_up = jnp.dot(row_tokens.T, up_grad, preferred_element_type=jnp.float32)
    grad_down = jnp.dot(hidden.T, out_grad, preferred_element_type=jnp.float32)
    return (grad_gate, grad_up, grad_down)


def expert_pass(weight_gate, weight_up, weight_down, row_tokens, row_cotan, row_weights):
    row_grads, pieces = forward_rows(
        weight_gate, weight_up, weight_down, row_tokens, row_cotan, row_weights
    )
    return (row_grads, weight_terms(pieces))


def shards(tokens, cotangent, routes, combine, hot_experts, extra_slots, w_gate, w_up, w_down):
    expert_count = lax.axis_size("expert")
    token_count, features = tokens.shape
    route_count = routes.shape[1]
    capacity = max(2, min(token_count * route_count * 7 // (8 * expert_count), token_count // 2))
    spare_slots = 2 * max(1, capacity // 6)
    expert_ids = routes.reshape(-1)
    assign_count = expert_ids.shape[0]
    assign_order = jnp.arange(assign_count, dtype=jnp.int32)
    earlier = (expert_ids[:, None] == expert_ids[None, :]) & (
        assign_order[None, :] < assign_order[:, None]
    )
    slot_rank = jnp.sum(earlier.astype(jnp.int32), axis=1)
    hot_match = expert_ids[:, None] == hot_experts[None, :]
    slot_limit = capacity + jnp.sum(jnp.where(hot_match, extra_slots[None, :], 0), axis=1)
    is_kept = slot_rank < slot_limit
    slot_count = capacity + spare_slots
    total_slots = expert_count * slot_count
    flat_slot = jnp.where(is_kept, expert_ids * slot_count + slot_rank, total_slots)
    slot_ids = jnp.arange(total_slots, dtype=jnp.int32)
    assign_onehot = slot_ids[:, None] == flat_slot[None, :]
    token_onehot = jnp.any(
        assign_onehot.reshape(total_slots, token_count, route_count), axis=2
    ).astype(jnp.bfloat16)
    both_rows = jnp.concatenate([tokens, cotangent], axis=1)
    filled = jnp.dot(token_onehot, both_rows, preferred_element_type=jnp.float32).astype(
        jnp.bfloat16
    )
    token_send = filled[:, :features].reshape(expert_count, slot_count, features)
    cotan_send = filled[:, features:].reshape(expert_count, slot_count, features)
    weight_flat = jnp.sum(
        jnp.where(assign_onehot, combine.reshape(-1).astype(jnp.float32)[None, :], 0.0), axis=1
    )
    weight_send = weight_flat.astype(jnp.bfloat16).reshape(expert_count, slot_count)
    token_recv, cotan_recv, weight_recv = (
        lax.all_to_all(token_send, "expert", split_axis=0, concat_axis=0, tiled=True),
        lax.all_to_all(cotan_send, "expert", split_axis=0, concat_axis=0, tiled=True),
        lax.all_to_all(weight_send, "expert", split_axis=0, concat_axis=0, tiled=True),
    )
    own_weights = (w_gate[0], w_up[0], w_down[0])
    all_rows, grad_terms = expert_pass(
        own_weights[0],
        own_weights[1],
        own_weights[2],
        token_recv.reshape(-1, features),
        cotan_recv.reshape(-1, features),
        weight_recv.reshape(-1),
    )
    grad_rows = all_rows.reshape(expert_count, slot_count, features)
    returned_rows = lax.all_to_all(grad_rows, "expert", split_axis=0, concat_axis=0, tiled=True)
    token_grads = jnp.dot(
        token_onehot.T,
        returned_rows.reshape(total_slots, features),
        preferred_element_type=jnp.float32,
    ).astype(jnp.bfloat16)
    grad_gate, grad_up = (
        lax.psum_scatter(grad_terms[0][None], "dp", scatter_dimension=1, tiled=True),
        lax.psum_scatter(grad_terms[1][None], "dp", scatter_dimension=1, tiled=True),
    )
    grad_down = lax.psum(grad_terms[2][None], "dp")
    return (
        token_grads,
        grad_gate.astype(jnp.bfloat16),
        grad_up.astype(jnp.bfloat16),
        grad_down.astype(jnp.bfloat16),
    )


MESH = pl.DeviceIdType.MESH
LANES = 128
TILE = 16
NT = (((1,), (1,)), ((), ()))
TN = (((0,), (0,)), ((), ()))


def slots_of(token_count, route_count, expert_count):
    capacity = max(2, min(token_count * route_count * 7 // (8 * expert_count), token_count // 2))
    return capacity, 2 * max(1, capacity // 6)


def dense_fits(sizes, token_count, features, route_count, hidden_size):
    capacity, spare = slots_of(token_count, route_count, sizes["expert"])
    return (
        route_count == sizes["expert"]
        and sizes["dp"] == 4
        and sizes["expert"] % 2 == 0
        and token_count == 2 * TILE
        and capacity == TILE
        and spare * 2 == 8
        and features % (8 * LANES) == 0
        and hidden_size % LANES == 0
    )


def dense_kernel(
    experts,
    tok_hbm,
    cot_hbm,
    routes_hbm,
    comb_hbm,
    hot_hbm,
    extra_hbm,
    wg_hbm,
    wu_hbm,
    wd_hbm,
    tg_ref,
    gg_out,
    gu_out,
    gd_out,
    tok_ref,
    cot_ref,
    routes_ref,
    comb_ref,
    hot_ref,
    extra_ref,
    in_sem,
    slab,
    wg,
    wu,
    wd,
    all_t,
    all_og,
    all_h,
    all_gg,
    all_ug,
    acc_gate,
    acc_up,
    acc_down,
    row_out,
    pair_in,
    pair_sum,
    z_in,
    w_sem,
    send_sem,
    recv_sem,
    pair_send,
    pair_recv,
    z_send,
    z_recv,
):
    levels = experts // 2
    features = tok_ref.shape[1]
    blocks = features // LANES
    half = blocks // 2
    spill_at = 2 * blocks
    weight_at = spill_at + half
    bf16, f32 = jnp.bfloat16, jnp.float32

    d = lax.axis_index("dp")
    e = lax.axis_index("expert")
    z, c = e // 2, e % 2
    dx = d + 1 - 2 * (d % 2)
    dy = (d + 2) % 4
    dd = 3 - d
    pc = 1 - c

    def to(dp, level, core):
        return (dp, level * 2 + core)

    def slab_id(dp, level, core):
        return dp * experts + level * 2 + core

    input_copies = [
        pltpu.make_async_copy(h, v, in_sem.at[i])
        for i, (h, v) in enumerate(
            (
                (tok_hbm, tok_ref),
                (cot_hbm, cot_ref),
                (routes_hbm, routes_ref),
                (comb_hbm, comb_ref),
                (hot_hbm, hot_ref),
                (extra_hbm, extra_ref),
            )
        )
    ]
    for copy in input_copies:
        copy.start()
    weight_copies = [
        pltpu.make_async_copy(h.at[0], v, w_sem.at[i])
        for i, (h, v) in enumerate(((wg_hbm, wg), (wu_hbm, wu), (wd_hbm, wd)))
    ]
    for copy in weight_copies:
        copy.start()

    barrier = pltpu.get_barrier_semaphore()
    for peer in (to(dx, z, c), to(dy, z, c), to(d, z, pc)):
        pl.semaphore_signal(barrier, inc=1, device_id=peer, device_id_type=MESH)
    for step in range(1, levels):
        pl.semaphore_signal(
            barrier, inc=1, device_id=to(d, (z + step) % levels, c), device_id_type=MESH
        )

    me = slab_id(d, z, c)
    for copy in input_copies:
        copy.wait()
    names = -(-experts // TILE) * TILE
    expert_row = lax.broadcasted_iota(jnp.int32, (names, 2 * TILE), 0)
    token_lane = lax.broadcasted_iota(jnp.int32, (names, 2 * TILE), 1)
    routes = routes_ref[...]
    comb = comb_ref[...].astype(f32)
    weights = jnp.zeros((names, 2 * TILE), f32)
    for r in range(routes.shape[0]):
        weights = jnp.where(expert_row == routes[r : r + 1, :], comb[r : r + 1, :], weights)
    limit = jnp.full((names, 2 * TILE), TILE, jnp.int32)
    for j in range(hot_ref.shape[0]):
        limit = limit + jnp.where(expert_row == hot_ref[j], extra_ref[j], 0)
    weights = jnp.where(token_lane < limit, weights, 0.0).astype(bf16)
    unit = lax.broadcasted_iota(jnp.int32, (names, LANES), 0) == lax.broadcasted_iota(
        jnp.int32, (names, LANES), 1
    )
    weights = lax.dot_general(
        weights, jnp.where(unit, 1.0, 0.0).astype(bf16), TN, preferred_element_type=f32
    ).astype(bf16)
    slab[me, weight_at] = weights[:TILE]
    slab[me, weight_at + 1] = weights[TILE:]
    tok_tail = tok_ref[TILE:, :].astype(f32)[:8]
    cot_tail = cot_ref[TILE:, :].astype(f32)[:8]
    tail_row = lax.broadcasted_iota(jnp.int32, (8, features), 0)
    spill = jnp.where(tail_row < 4, tok_tail, pltpu.roll(cot_tail, 4, 0))
    for j in range(blocks):
        cols = slice(j * LANES, (j + 1) * LANES)
        slab[me, j] = tok_ref[:TILE, cols]
        slab[me, blocks + j] = cot_ref[:TILE, cols]
    for j in range(half):
        lo = spill[:, j * LANES : (j + 1) * LANES]
        hi = spill[:, (half + j) * LANES : (half + j + 1) * LANES]
        slab[me, spill_at + j] = jnp.concatenate([lo, hi], axis=0).astype(bf16)

    pl.semaphore_wait(barrier, 3 + levels - 1)

    def copy_of(s, way, peer):
        return pltpu.make_async_remote_copy(
            src_ref=slab.at[s],
            dst_ref=slab.at[s],
            send_sem=send_sem.at[way, s],
            recv_sem=recv_sem.at[s],
            device_id=peer,
            device_id_type=MESH,
        )

    def to_x(s):
        return copy_of(s, 0, to(dx, z, c))

    def to_y(s):
        return copy_of(s, 1, to(dy, z, c))

    def to_pair(s):
        return copy_of(s, 2, to(d, z, pc))

    def to_up(s):
        return copy_of(s, 3, to(d, z + 1, c))

    def to_down(s):
        return copy_of(s, 4, to(d, z - 1, c))

    def arrived(s):
        to_pair(s).wait_recv()

    @pl.when(z + 1 < levels)
    def _():
        to_up(me).start()

    @pl.when(z > 0)
    def _():
        to_down(me).start()

    to_x(me).start()
    to_y(me).start()
    to_pair(me).start()

    for dist in range(1, levels):

        @pl.when(z - dist >= 0)
        def _():
            s = slab_id(d, z - dist, c)
            arrived(s)

            @pl.when(z + 1 < levels)
            def _():
                to_up(s).start()

            to_x(s).start()
            to_y(s).start()
            to_pair(s).start()

        @pl.when(z + dist < levels)
        def _():
            s = slab_id(d, z + dist, c)
            arrived(s)

            @pl.when(z > 0)
            def _():
                to_down(s).start()

            to_x(s).start()
            to_y(s).start()
            to_pair(s).start()

    for level in range(levels):
        arrived(slab_id(d, level, pc))

    main_rows = experts * TILE
    group_rows = main_rows + experts * 8
    own_lane = lax.broadcasted_iota(jnp.int32, (group_rows, LANES), 1) == e

    def group(dp, at):
        rows = pl.ds(at, group_rows)
        part = pl.ds(dp * experts, experts)

        def main(j):
            return slab[part, j].reshape(main_rows, LANES)

        lo, hi = [], []
        for j in range(half):
            both = slab[part, spill_at + j].astype(f32)
            lo.append(both[:, :8].reshape(experts * 8, LANES))
            hi.append(both[:, 8:].reshape(experts * 8, LANES))
        tail = jnp.concatenate(lo + hi, axis=1)
        cot_rows = pltpu.roll(tail, experts * 8 - 4, 0)
        w_main = main(weight_at).astype(f32)
        w_tail = slab[part, weight_at + 1].astype(f32)[:, :8].reshape(experts * 8, LANES)
        w = jnp.sum(
            jnp.where(own_lane, jnp.concatenate([w_main, w_tail], axis=0), 0.0),
            axis=1,
            keepdims=True,
        )
        all_t[rows, :] = jnp.concatenate(
            [jnp.concatenate([main(j) for j in range(blocks)], axis=1), tail.astype(bf16)], axis=0
        )
        cot = jnp.concatenate(
            [
                jnp.concatenate([main(blocks + j) for j in range(blocks)], axis=1).astype(f32),
                cot_rows,
            ],
            axis=0,
        )
        all_og[rows, :] = (w * cot).astype(bf16)
        t = all_t[rows, :]
        gate_pre = jnp.dot(t, wg[...], preferred_element_type=f32)
        up_proj = jnp.dot(t, wu[...], preferred_element_type=f32)
        hidden_grad = lax.dot_general(all_og[rows, :], wd[...], NT, preferred_element_type=f32)
        sig = jax.nn.sigmoid(gate_pre)
        act = gate_pre * sig
        all_h[rows, :] = (act * up_proj).astype(bf16)
        all_gg[rows, :] = (hidden_grad * up_proj * sig * (1.0 + gate_pre * (1.0 - sig))).astype(
            bf16
        )
        all_ug[rows, :] = (hidden_grad * act).astype(bf16)

    for copy in weight_copies:
        copy.wait()
    group(d, 0)
    own = pl.ds(0, group_rows)
    rg = lax.dot_general(all_gg[own, :], wg[...], NT, preferred_element_type=f32)
    rg = rg + lax.dot_general(all_ug[own, :], wu[...], NT, preferred_element_type=f32)
    for j in range(blocks):
        row_out[:, j] = (
            rg[:main_rows, j * LANES : (j + 1) * LANES].reshape(experts, TILE, LANES).astype(bf16)
        )
    for j in range(half):
        lo = rg[main_rows:, j * LANES : (j + 1) * LANES].reshape(experts, 8, LANES)
        hi = rg[main_rows:, (half + j) * LANES : (half + j + 1) * LANES].reshape(experts, 8, LANES)
        row_out[:, blocks + j] = jnp.concatenate([lo, hi], axis=1).astype(bf16)

    def pair_copy(level):
        return pltpu.make_async_remote_copy(
            src_ref=row_out.at[level * 2 + pc],
            dst_ref=pair_in.at[level],
            send_sem=pair_send.at[level],
            recv_sem=pair_recv.at[level],
            device_id=to(d, z, pc),
            device_id_type=MESH,
        )

    for level in range(levels):
        pair_copy(level).start()

    for level in range(levels):
        s = slab_id(dx, level, c)
        arrived(s)
        if level % 2 == 0:
            to_y(s).start()
        to_pair(s).start()
        s = slab_id(dy, level, c)
        arrived(s)
        if level % 2 == 1:
            to_x(s).start()
        to_pair(s).start()

    for level in range(levels):
        pair_copy(level).wait_recv()
        pair_sum[level] = (
            row_out[level * 2 + c].astype(f32) + pair_in[level].astype(f32)
        ).astype(bf16)

    def z_copy(step):
        level = (z + step) % levels
        return pltpu.make_async_remote_copy(
            src_ref=pair_sum.at[level],
            dst_ref=z_in.at[step - 1],
            send_sem=z_send.at[step - 1],
            recv_sem=z_recv.at[step - 1],
            device_id=to(d, level, c),
            device_id_type=MESH,
        )

    for step in range(1, levels):
        z_copy(step).start()

    for level in range(levels):
        arrived(slab_id(dx, level, pc))
    group(dx, group_rows)
    for level in range(levels):
        s = slab_id(dd, level, c)
        arrived(s)
        to_pair(s).start()
    for level in range(levels):
        arrived(slab_id(dy, level, pc))
    group(dy, 2 * group_rows)
    share = features // 4

    def weight_terms(at, count):
        rows = pl.ds(at, count)
        t_cols = all_t[rows, pl.ds(pl.multiple_of(d * share, LANES), share)]
        return (
            lax.dot_general(t_cols, all_gg[rows, :], TN, preferred_element_type=f32),
            lax.dot_general(t_cols, all_ug[rows, :], TN, preferred_element_type=f32),
            lax.dot_general(all_h[rows, :], all_og[rows, :], TN, preferred_element_type=f32),
        )

    early = weight_terms(0, 3 * group_rows)
    acc_gate[...], acc_up[...], acc_down[...] = early
    for level in range(levels):
        arrived(slab_id(dd, level, pc))
    group(dd, 3 * group_rows)
    late = weight_terms(3 * group_rows, group_rows)
    gg_out[0] = (acc_gate[...] + late[0]).astype(bf16)
    gu_out[0] = (acc_up[...] + late[1]).astype(bf16)
    gd_out[0] = (acc_down[...] + late[2]).astype(bf16)

    total = pair_sum[z].astype(f32)
    for step in range(1, levels):
        z_copy(step).wait_recv()
        total = total + z_in[step - 1].astype(f32)
    for j in range(blocks):
        tg_ref[:TILE, j * LANES : (j + 1) * LANES] = total[j].astype(bf16)
    blank = jnp.zeros((8, LANES), f32)
    for j in range(half):
        tile = total[blocks + j]
        tg_ref[TILE:, j * LANES : (j + 1) * LANES] = jnp.concatenate(
            [tile[:8], blank], axis=0
        ).astype(bf16)
        tg_ref[TILE:, (half + j) * LANES : (half + j + 1) * LANES] = jnp.concatenate(
            [tile[8:], blank], axis=0
        ).astype(bf16)

    for level in range(levels):
        s = slab_id(d, level, c)
        to_x(s).wait_send()
        to_y(s).wait_send()
        to_pair(s).wait_send()
        if level % 2 == 0:
            to_y(slab_id(dx, level, c)).wait_send()
        else:
            to_x(slab_id(dy, level, c)).wait_send()
        for dp in (dx, dy, dd):
            to_pair(slab_id(dp, level, c)).wait_send()
        pair_copy(level).wait_send()

        @pl.when((z >= level) & (z + 1 < levels))
        def _():
            to_up(s).wait_send()

        @pl.when((z <= level) & (z > 0))
        def _():
            to_down(s).wait_send()

    for step in range(1, levels):
        z_copy(step).wait_send()


def write_kernel(*refs):
    sources, sem = refs[: len(refs) // 2], refs[-1]
    targets = refs[len(refs) // 2 : -1]
    copies = [
        pltpu.make_async_copy(a, b, sem.at[i]) for i, (a, b) in enumerate(zip(sources, targets))
    ]
    for copy in copies:
        copy.start()
    for copy in copies:
        copy.wait()


def dense_shards(tokens, cotangent, routes, combine, hot_experts, extra_slots, w_gate, w_up, w_down):
    experts = lax.axis_size("expert")
    replicas = lax.axis_size("dp")
    token_count, features = tokens.shape
    hidden_size = w_gate.shape[2]
    blocks = features // LANES
    levels = experts // 2
    tiles = 2 * blocks + blocks // 2 + 2
    back = blocks + blocks // 2
    rows = replicas * experts * (TILE + 8)
    bf16 = jnp.bfloat16
    vmem = pl.BlockSpec(memory_space=pltpu.VMEM)
    hbm = pl.BlockSpec(memory_space=pltpu.HBM)
    dma = pltpu.SemaphoreType.DMA
    operands = [
        pltpu.with_memory_space_constraint(a, pltpu.HBM)
        for a in (
            tokens,
            cotangent,
            routes.T,
            combine.T,
            hot_experts,
            extra_slots,
            w_gate,
            w_up,
            w_down,
        )
    ]
    results = pl.pallas_call(
        functools.partial(dense_kernel, experts),
        out_shape=(
            jax.ShapeDtypeStruct((token_count, features), bf16),
            jax.ShapeDtypeStruct((1, features // replicas, hidden_size), bf16),
            jax.ShapeDtypeStruct((1, features // replicas, hidden_size), bf16),
            jax.ShapeDtypeStruct((1, hidden_size, features), bf16),
        ),
        in_specs=[hbm] * 9,
        out_specs=(vmem, vmem, vmem, vmem),
        scratch_shapes=[
            pltpu.VMEM(tokens.shape, bf16),
            pltpu.VMEM(tokens.shape, bf16),
            pltpu.VMEM(routes.shape[::-1], jnp.int32),
            pltpu.VMEM(routes.shape[::-1], bf16),
            pltpu.SMEM(hot_experts.shape, jnp.int32),
            pltpu.SMEM(hot_experts.shape, jnp.int32),
            dma((6,)),
            pltpu.VMEM((replicas * experts, tiles, TILE, LANES), bf16),
            pltpu.VMEM((features, hidden_size), bf16),
            pltpu.VMEM((features, hidden_size), bf16),
            pltpu.VMEM((hidden_size, features), bf16),
            pltpu.VMEM((rows, features), bf16),
            pltpu.VMEM((rows, features), bf16),
            pltpu.VMEM((rows, hidden_size), bf16),
            pltpu.VMEM((rows, hidden_size), bf16),
            pltpu.VMEM((rows, hidden_size), bf16),
            pltpu.VMEM((features // replicas, hidden_size), jnp.float32),
            pltpu.VMEM((features // replicas, hidden_size), jnp.float32),
            pltpu.VMEM((hidden_size, features), jnp.float32),
            pltpu.VMEM((experts, back, TILE, LANES), bf16),
            pltpu.VMEM((levels, back, TILE, LANES), bf16),
            pltpu.VMEM((levels, back, TILE, LANES), bf16),
            pltpu.VMEM((levels - 1, back, TILE, LANES), bf16),
            dma((3,)),
            dma((5, replicas * experts)),
            dma((replicas * experts,)),
            dma((levels,)),
            dma((levels,)),
            dma((levels - 1,)),
            dma((levels - 1,)),
        ],
        compiler_params=pltpu.CompilerParams(
            collective_id=0, has_side_effects=True, vmem_limit_bytes=32 * 1024 * 1024
        ),
    )(*operands)
    return pl.pallas_call(
        write_kernel,
        out_shape=tuple(jax.ShapeDtypeStruct(r.shape, r.dtype) for r in results),
        in_specs=[vmem] * len(results),
        out_specs=tuple(hbm for _ in results),
        scratch_shapes=[dma((len(results),))],
        compiler_params=pltpu.CompilerParams(vmem_limit_bytes=8 * 1024 * 1024),
    )(*results)


def solution(mesh):
    in_specs = (
        P(("dp", "expert"), None),
        P(("dp", "expert"), None),
        P(("dp", "expert"), None),
        P(("dp", "expert"), None),
        P(),
        P(),
        P("expert", None, None),
        P("expert", None, None),
        P("expert", None, None),
    )
    out_specs = (
        P(("dp", "expert"), None),
        P("expert", "dp", None),
        P("expert", "dp", None),
        P("expert", None, None),
    )

    def body(*args):
        token_count, features = args[0].shape
        if dense_fits(dict(mesh.shape), token_count, features, args[2].shape[1], args[6].shape[2]):
            return dense_shards(*args)
        return shards(*args)

    return jax.shard_map(body, mesh=mesh, in_specs=in_specs, out_specs=out_specs, check_vma=False)
```

```python
import functools

import jax
import jax.numpy as jnp
from jax import lax
from jax.experimental import pallas as pl
from jax.experimental.pallas import tpu as pltpu
from jax.sharding import PartitionSpec as P


def forward_rows(weight_gate, weight_up, weight_down, row_tokens, row_cotan, row_weights):
    gate_pre = jnp.dot(row_tokens, weight_gate, preferred_element_type=jnp.float32)
    up_proj = jnp.dot(row_tokens, weight_up, preferred_element_type=jnp.float32)
    sigmoid_gate = jax.nn.sigmoid(gate_pre)
    gate_act = gate_pre * sigmoid_gate
    hidden = (gate_act * up_proj).astype(jnp.bfloat16)
    out_grad = (row_weights.astype(jnp.float32)[:, None] * row_cotan.astype(jnp.float32)).astype(
        jnp.bfloat16
    )
    hidden_grad = jnp.dot(out_grad, weight_down.T, preferred_element_type=jnp.float32)
    gate_grad = (
        hidden_grad * up_proj * sigmoid_gate * (1.0 + gate_pre * (1.0 - sigmoid_gate))
    ).astype(jnp.bfloat16)
    up_grad = (hidden_grad * gate_act).astype(jnp.bfloat16)
    row_grads = jnp.dot(gate_grad, weight_gate.T, preferred_element_type=jnp.float32)
    row_grads = row_grads + jnp.dot(up_grad, weight_up.T, preferred_element_type=jnp.float32)
    return (row_grads.astype(jnp.bfloat16), (row_tokens, gate_grad, up_grad, hidden, out_grad))


def weight_terms(pieces):
    row_tokens, gate_grad, up_grad, hidden, out_grad = pieces
    grad_gate = jnp.dot(row_tokens.T, gate_grad, preferred_element_type=jnp.float32)
    grad_up = jnp.dot(row_tokens.T, up_grad, preferred_element_type=jnp.float32)
    grad_down = jnp.dot(hidden.T, out_grad, preferred_element_type=jnp.float32)
    return (grad_gate, grad_up, grad_down)


def expert_pass(weight_gate, weight_up, weight_down, row_tokens, row_cotan, row_weights):
    row_grads, pieces = forward_rows(
        weight_gate, weight_up, weight_down, row_tokens, row_cotan, row_weights
    )
    return (row_grads, weight_terms(pieces))


def shards(tokens, cotangent, routes, combine, hot_experts, extra_slots, w_gate, w_up, w_down):
    expert_count = lax.axis_size("expert")
    token_count, features = tokens.shape
    route_count = routes.shape[1]
    capacity = max(2, min(token_count * route_count * 7 // (8 * expert_count), token_count // 2))
    spare_slots = 2 * max(1, capacity // 6)
    expert_ids = routes.reshape(-1)
    assign_count = expert_ids.shape[0]
    assign_order = jnp.arange(assign_count, dtype=jnp.int32)
    earlier = (expert_ids[:, None] == expert_ids[None, :]) & (
        assign_order[None, :] < assign_order[:, None]
    )
    slot_rank = jnp.sum(earlier.astype(jnp.int32), axis=1)
    hot_match = expert_ids[:, None] == hot_experts[None, :]
    slot_limit = capacity + jnp.sum(jnp.where(hot_match, extra_slots[None, :], 0), axis=1)
    is_kept = slot_rank < slot_limit
    slot_count = capacity + spare_slots
    total_slots = expert_count * slot_count
    flat_slot = jnp.where(is_kept, expert_ids * slot_count + slot_rank, total_slots)
    slot_ids = jnp.arange(total_slots, dtype=jnp.int32)
    assign_onehot = slot_ids[:, None] == flat_slot[None, :]
    token_onehot = jnp.any(
        assign_onehot.reshape(total_slots, token_count, route_count), axis=2
    ).astype(jnp.bfloat16)
    both_rows = jnp.concatenate([tokens, cotangent], axis=1)
    filled = jnp.dot(token_onehot, both_rows, preferred_element_type=jnp.float32).astype(
        jnp.bfloat16
    )
    token_send = filled[:, :features].reshape(expert_count, slot_count, features)
    cotan_send = filled[:, features:].reshape(expert_count, slot_count, features)
    weight_flat = jnp.sum(
        jnp.where(assign_onehot, combine.reshape(-1).astype(jnp.float32)[None, :], 0.0), axis=1
    )
    weight_send = weight_flat.astype(jnp.bfloat16).reshape(expert_count, slot_count)
    token_recv, cotan_recv, weight_recv = (
        lax.all_to_all(token_send, "expert", split_axis=0, concat_axis=0, tiled=True),
        lax.all_to_all(cotan_send, "expert", split_axis=0, concat_axis=0, tiled=True),
        lax.all_to_all(weight_send, "expert", split_axis=0, concat_axis=0, tiled=True),
    )
    own_weights = (w_gate[0], w_up[0], w_down[0])
    all_rows, grad_terms = expert_pass(
        own_weights[0],
        own_weights[1],
        own_weights[2],
        token_recv.reshape(-1, features),
        cotan_recv.reshape(-1, features),
        weight_recv.reshape(-1),
    )
    grad_rows = all_rows.reshape(expert_count, slot_count, features)
    returned_rows = lax.all_to_all(grad_rows, "expert", split_axis=0, concat_axis=0, tiled=True)
    token_grads = jnp.dot(
        token_onehot.T,
        returned_rows.reshape(total_slots, features),
        preferred_element_type=jnp.float32,
    ).astype(jnp.bfloat16)
    grad_gate, grad_up = (
        lax.psum_scatter(grad_terms[0][None], "dp", scatter_dimension=1, tiled=True),
        lax.psum_scatter(grad_terms[1][None], "dp", scatter_dimension=1, tiled=True),
    )
    grad_down = lax.psum(grad_terms[2][None], "dp")
    return (
        token_grads,
        grad_gate.astype(jnp.bfloat16),
        grad_up.astype(jnp.bfloat16),
        grad_down.astype(jnp.bfloat16),
    )


MESH = pl.DeviceIdType.MESH
LANES = 128
TILE = 16
NT = (((1,), (1,)), ((), ()))
TN = (((0,), (0,)), ((), ()))


def slots_of(token_count, route_count, expert_count):
    capacity = max(2, min(token_count * route_count * 7 // (8 * expert_count), token_count // 2))
    return capacity, 2 * max(1, capacity // 6)


def dense_fits(sizes, token_count, features, route_count, hidden_size):
    capacity, spare = slots_of(token_count, route_count, sizes["expert"])
    return (
        route_count == sizes["expert"]
        and sizes["dp"] == 4
        and sizes["expert"] % 2 == 0
        and token_count == 2 * TILE
        and capacity == TILE
        and spare * 2 == 8
        and features % (8 * LANES) == 0
        and hidden_size % LANES == 0
    )


def dense_kernel(
    experts,
    tok_hbm,
    cot_hbm,
    routes_hbm,
    comb_hbm,
    hot_hbm,
    extra_hbm,
    wg_hbm,
    wu_hbm,
    wd_hbm,
    tg_ref,
    gg_out,
    gu_out,
    gd_out,
    tok_ref,
    cot_ref,
    routes_ref,
    comb_ref,
    hot_ref,
    extra_ref,
    in_sem,
    slab,
    wg,
    wu,
    wd,
    all_t,
    all_og,
    all_h,
    all_gg,
    all_ug,
    acc_gate,
    acc_up,
    acc_down,
    row_out,
    pair_in,
    pair_sum,
    z_in,
    w_sem,
    send_sem,
    recv_sem,
    pair_send,
    pair_recv,
    z_send,
    z_recv,
):
    levels = experts // 2
    features = tok_ref.shape[1]
    blocks = features // LANES
    half = blocks // 2
    spill_at = 2 * blocks
    weight_at = spill_at + half
    bf16, f32 = jnp.bfloat16, jnp.float32

    d = lax.axis_index("dp")
    e = lax.axis_index("expert")
    z, c = e // 2, e % 2
    dx = d + 1 - 2 * (d % 2)
    dy = (d + 2) % 4
    dd = 3 - d
    pc = 1 - c

    def to(dp, level, core):
        return (dp, level * 2 + core)

    def slab_id(dp, level, core):
        return dp * experts + level * 2 + core

    input_copies = [
        pltpu.make_async_copy(h, v, in_sem.at[i])
        for i, (h, v) in enumerate(
            (
                (tok_hbm, tok_ref),
                (cot_hbm, cot_ref),
                (routes_hbm, routes_ref),
                (comb_hbm, comb_ref),
                (hot_hbm, hot_ref),
                (extra_hbm, extra_ref),
            )
        )
    ]
    for copy in input_copies:
        copy.start()
    weight_copies = [
        pltpu.make_async_copy(h.at[0], v, w_sem.at[i])
        for i, (h, v) in enumerate(((wg_hbm, wg), (wu_hbm, wu), (wd_hbm, wd)))
    ]
    for copy in weight_copies:
        copy.start()

    barrier = pltpu.get_barrier_semaphore()
    for peer in (to(dx, z, c), to(dy, z, c), to(d, z, pc)):
        pl.semaphore_signal(barrier, inc=1, device_id=peer, device_id_type=MESH)
    for step in range(1, levels):
        pl.semaphore_signal(
            barrier, inc=1, device_id=to(d, (z + step) % levels, c), device_id_type=MESH
        )

    me = slab_id(d, z, c)
    for copy in input_copies:
        copy.wait()
    names = -(-experts // TILE) * TILE
    expert_row = lax.broadcasted_iota(jnp.int32, (names, 2 * TILE), 0)
    token_lane = lax.broadcasted_iota(jnp.int32, (names, 2 * TILE), 1)
    routes = routes_ref[...]
    comb = comb_ref[...].astype(f32)
    weights = jnp.zeros((names, 2 * TILE), f32)
    for r in range(routes.shape[0]):
        weights = jnp.where(expert_row == routes[r : r + 1, :], comb[r : r + 1, :], weights)
    limit = jnp.full((names, 2 * TILE), TILE, jnp.int32)
    for j in range(hot_ref.shape[0]):
        limit = limit + jnp.where(expert_row == hot_ref[j], extra_ref[j], 0)
    weights = jnp.where(token_lane < limit, weights, 0.0).astype(bf16)
    unit_row = lax.broadcasted_iota(jnp.int32, (names, LANES), 0)
    unit_lane = lax.broadcasted_iota(jnp.int32, (names, LANES), 1)

    def turned(shift):
        unit = jnp.where(unit_lane == unit_row + shift, 1.0, 0.0).astype(bf16)
        return lax.dot_general(weights, unit, TN, preferred_element_type=f32)

    main_part, tail_part = turned(0), turned(LANES // 2)
    slab[me, weight_at] = (main_part[:TILE] + tail_part[TILE:]).astype(bf16)
    tok_tail = tok_ref[TILE:, :].astype(f32)[:8]
    cot_tail = cot_ref[TILE:, :].astype(f32)[:8]
    tail_row = lax.broadcasted_iota(jnp.int32, (8, features), 0)
    spill = jnp.where(tail_row < 4, tok_tail, pltpu.roll(cot_tail, 4, 0))
    for j in range(blocks):
        cols = slice(j * LANES, (j + 1) * LANES)
        slab[me, j] = tok_ref[:TILE, cols]
        slab[me, blocks + j] = cot_ref[:TILE, cols]
    for j in range(half):
        lo = spill[:, j * LANES : (j + 1) * LANES]
        hi = spill[:, (half + j) * LANES : (half + j + 1) * LANES]
        slab[me, spill_at + j] = jnp.concatenate([lo, hi], axis=0).astype(bf16)

    pl.semaphore_wait(barrier, 3 + levels - 1)

    tiles = slab.shape[1]
    cut = (tiles + 1) // 2
    pieces = (pl.ds(0, cut), pl.ds(cut, tiles - cut))

    def copy_of(s, p, way, peer):
        return pltpu.make_async_remote_copy(
            src_ref=slab.at[s, pieces[p]],
            dst_ref=slab.at[s, pieces[p]],
            send_sem=send_sem.at[way, p, s],
            recv_sem=recv_sem.at[p, s],
            device_id=peer,
            device_id_type=MESH,
        )

    def to_x(s, p):
        return copy_of(s, p, 0, to(dx, z, c))

    def to_y(s, p):
        return copy_of(s, p, 1, to(dy, z, c))

    def to_pair(s, p):
        return copy_of(s, p, 2, to(d, z, pc))

    def to_level(p, step):
        return copy_of(me, p, 2 + step, to(d, (z + step) % levels, c))

    def arrived(s, p):
        to_pair(s, p).wait_recv()

    def at_distance(dist, visit):
        if dist == 0:
            visit(z, 0)
            return
        pl.when(z - dist >= 0)(lambda: visit(z - dist, -1))
        pl.when(z + dist < levels)(lambda: visit(z + dist, 1))

    def column(dist, p):
        def visit(level, side):
            s = slab_id(d, level, c)
            if side:
                arrived(s, p)
            to_x(s, p).start()
            to_y(s, p).start()
            if side == 0:
                for step in range(1, levels):
                    to_level(p, step).start()
            to_pair(s, p).start()

        at_distance(dist, visit)

    def beside(dist, p):
        def visit(level, side):
            for dp in (dx, dy):
                s = slab_id(dp, level, c)
                arrived(s, p)
                if p == 0 and dp is dx:
                    to_y(s, p).start()
                if p == 1 and dp is dy:
                    to_x(s, p).start()
                to_pair(s, p).start()

        at_distance(dist, visit)

    def across(dist):
        def visit(level, side):
            s = slab_id(dd, level, c)
            for p in (0, 1):
                arrived(s, p)
                to_pair(s, p).start()

        at_distance(dist, visit)

    def from_pair(dp):
        for level in range(levels):
            for p in (0, 1):
                arrived(slab_id(dp, level, pc), p)

    column(0, 0)
    column(0, 1)
    for dist in range(1, levels):
        for p in (0, 1):
            column(dist, p)
    from_pair(d)

    main_rows = experts * TILE
    group_rows = main_rows + experts * 8
    main_lane = lax.broadcasted_iota(jnp.int32, (main_rows, LANES), 1)
    tail_lane = lax.broadcasted_iota(jnp.int32, (experts * 8, LANES), 1)

    def group(dp, at):
        rows = pl.ds(at, group_rows)
        part = pl.ds(dp * experts, experts)

        def main(j):
            return slab[part, j].reshape(main_rows, LANES)

        lo, hi = [], []
        for j in range(half):
            both = slab[part, spill_at + j].astype(f32)
            lo.append(both[:, :8].reshape(experts * 8, LANES))
            hi.append(both[:, 8:].reshape(experts * 8, LANES))
        tail = jnp.concatenate(lo + hi, axis=1)
        cot_rows = pltpu.roll(tail, experts * 8 - 4, 0)
        w_all = slab[part, weight_at].astype(f32)
        w_main = w_all.reshape(main_rows, LANES)
        w_tail = w_all[:, :8].reshape(experts * 8, LANES)
        w = jnp.concatenate(
            [
                jnp.sum(jnp.where(main_lane == e, w_main, 0.0), axis=1, keepdims=True),
                jnp.sum(jnp.where(tail_lane == e + LANES // 2, w_tail, 0.0), axis=1, keepdims=True),
            ],
            axis=0,
        )
        all_t[rows, :] = jnp.concatenate(
            [jnp.concatenate([main(j) for j in range(blocks)], axis=1), tail.astype(bf16)], axis=0
        )
        cot = jnp.concatenate(
            [
                jnp.concatenate([main(blocks + j) for j in range(blocks)], axis=1).astype(f32),
                cot_rows,
            ],
            axis=0,
        )
        all_og[rows, :] = (w * cot).astype(bf16)
        t = all_t[rows, :]
        gate_pre = jnp.dot(t, wg[...], preferred_element_type=f32)
        up_proj = jnp.dot(t, wu[...], preferred_element_type=f32)
        hidden_grad = lax.dot_general(all_og[rows, :], wd[...], NT, preferred_element_type=f32)
        sig = jax.nn.sigmoid(gate_pre)
        act = gate_pre * sig
        all_h[rows, :] = (act * up_proj).astype(bf16)
        all_gg[rows, :] = (hidden_grad * up_proj * sig * (1.0 + gate_pre * (1.0 - sig))).astype(
            bf16
        )
        all_ug[rows, :] = (hidden_grad * act).astype(bf16)

    for copy in weight_copies:
        copy.wait()
    group(d, 0)
    own = pl.ds(0, group_rows)
    rg = lax.dot_general(all_gg[own, :], wg[...], NT, preferred_element_type=f32)
    rg = rg + lax.dot_general(all_ug[own, :], wu[...], NT, preferred_element_type=f32)
    for j in range(blocks):
        row_out[:, j] = (
            rg[:main_rows, j * LANES : (j + 1) * LANES].reshape(experts, TILE, LANES).astype(bf16)
        )
    for j in range(half):
        lo = rg[main_rows:, j * LANES : (j + 1) * LANES].reshape(experts, 8, LANES)
        hi = rg[main_rows:, (half + j) * LANES : (half + j + 1) * LANES].reshape(experts, 8, LANES)
        row_out[:, blocks + j] = jnp.concatenate([lo, hi], axis=1).astype(bf16)

    def pair_copy(level):
        return pltpu.make_async_remote_copy(
            src_ref=row_out.at[level * 2 + pc],
            dst_ref=pair_in.at[level],
            send_sem=pair_send.at[level],
            recv_sem=pair_recv.at[level],
            device_id=to(d, z, pc),
            device_id_type=MESH,
        )

    for level in range(levels):
        pair_copy(level).start()

    for dist in range(levels):
        for p in (0, 1):
            beside(dist, p)

    for level in range(levels):
        pair_copy(level).wait_recv()
        pair_sum[level] = (
            row_out[level * 2 + c].astype(f32) + pair_in[level].astype(f32)
        ).astype(bf16)

    def z_copy(step):
        level = (z + step) % levels
        return pltpu.make_async_remote_copy(
            src_ref=pair_sum.at[level],
            dst_ref=z_in.at[step - 1],
            send_sem=z_send.at[step - 1],
            recv_sem=z_recv.at[step - 1],
            device_id=to(d, level, c),
            device_id_type=MESH,
        )

    for step in range(1, levels):
        z_copy(step).start()

    from_pair(dx)
    group(dx, group_rows)
    from_pair(dy)
    group(dy, 2 * group_rows)
    for dist in range(levels):
        across(dist)
    share = features // 4

    def weight_terms(at, count):
        rows = pl.ds(at, count)
        t_cols = all_t[rows, pl.ds(pl.multiple_of(d * share, LANES), share)]
        return (
            lax.dot_general(t_cols, all_gg[rows, :], TN, preferred_element_type=f32),
            lax.dot_general(t_cols, all_ug[rows, :], TN, preferred_element_type=f32),
            lax.dot_general(all_h[rows, :], all_og[rows, :], TN, preferred_element_type=f32),
        )

    early = weight_terms(0, 3 * group_rows)
    acc_gate[...], acc_up[...], acc_down[...] = early
    from_pair(dd)
    group(dd, 3 * group_rows)
    late = weight_terms(3 * group_rows, group_rows)
    gg_out[0] = (acc_gate[...] + late[0]).astype(bf16)
    gu_out[0] = (acc_up[...] + late[1]).astype(bf16)
    gd_out[0] = (acc_down[...] + late[2]).astype(bf16)

    total = pair_sum[z].astype(f32)
    for step in range(1, levels):
        z_copy(step).wait_recv()
        total = total + z_in[step - 1].astype(f32)
    for j in range(blocks):
        tg_ref[:TILE, j * LANES : (j + 1) * LANES] = total[j].astype(bf16)
    blank = jnp.zeros((8, LANES), f32)
    for j in range(half):
        tile = total[blocks + j]
        tg_ref[TILE:, j * LANES : (j + 1) * LANES] = jnp.concatenate(
            [tile[:8], blank], axis=0
        ).astype(bf16)
        tg_ref[TILE:, (half + j) * LANES : (half + j + 1) * LANES] = jnp.concatenate(
            [tile[8:], blank], axis=0
        ).astype(bf16)

    for level in range(levels):
        pair_copy(level).wait_send()
        to_y(slab_id(dx, level, c), 0).wait_send()
        to_x(slab_id(dy, level, c), 1).wait_send()
        s = slab_id(d, level, c)
        for p in (0, 1):
            to_x(s, p).wait_send()
            to_y(s, p).wait_send()
            for dp in (d, dx, dy, dd):
                to_pair(slab_id(dp, level, c), p).wait_send()

    for step in range(1, levels):
        z_copy(step).wait_send()
        to_level(0, step).wait_send()
        to_level(1, step).wait_send()


def write_kernel(*refs):
    sources, sem = refs[: len(refs) // 2], refs[-1]
    targets = refs[len(refs) // 2 : -1]
    copies = [
        pltpu.make_async_copy(a, b, sem.at[i]) for i, (a, b) in enumerate(zip(sources, targets))
    ]
    for copy in copies:
        copy.start()
    for copy in copies:
        copy.wait()


def dense_shards(tokens, cotangent, routes, combine, hot_experts, extra_slots, w_gate, w_up, w_down):
    experts = lax.axis_size("expert")
    replicas = lax.axis_size("dp")
    token_count, features = tokens.shape
    hidden_size = w_gate.shape[2]
    blocks = features // LANES
    levels = experts // 2
    tiles = 2 * blocks + blocks // 2 + 1
    back = blocks + blocks // 2
    rows = replicas * experts * (TILE + 8)
    bf16 = jnp.bfloat16
    vmem = pl.BlockSpec(memory_space=pltpu.VMEM)
    hbm = pl.BlockSpec(memory_space=pltpu.HBM)
    dma = pltpu.SemaphoreType.DMA
    operands = [
        pltpu.with_memory_space_constraint(a, pltpu.HBM)
        for a in (
            tokens,
            cotangent,
            routes.T,
            combine.T,
            hot_experts,
            extra_slots,
            w_gate,
            w_up,
            w_down,
        )
    ]
    results = pl.pallas_call(
        functools.partial(dense_kernel, experts),
        out_shape=(
            jax.ShapeDtypeStruct((token_count, features), bf16),
            jax.ShapeDtypeStruct((1, features // replicas, hidden_size), bf16),
            jax.ShapeDtypeStruct((1, features // replicas, hidden_size), bf16),
            jax.ShapeDtypeStruct((1, hidden_size, features), bf16),
        ),
        in_specs=[hbm] * 9,
        out_specs=(vmem, vmem, vmem, vmem),
        scratch_shapes=[
            pltpu.VMEM(tokens.shape, bf16),
            pltpu.VMEM(tokens.shape, bf16),
            pltpu.VMEM(routes.shape[::-1], jnp.int32),
            pltpu.VMEM(routes.shape[::-1], bf16),
            pltpu.SMEM(hot_experts.shape, jnp.int32),
            pltpu.SMEM(hot_experts.shape, jnp.int32),
            dma((6,)),
            pltpu.VMEM((replicas * experts, tiles, TILE, LANES), bf16),
            pltpu.VMEM((features, hidden_size), bf16),
            pltpu.VMEM((features, hidden_size), bf16),
            pltpu.VMEM((hidden_size, features), bf16),
            pltpu.VMEM((rows, features), bf16),
            pltpu.VMEM((rows, features), bf16),
            pltpu.VMEM((rows, hidden_size), bf16),
            pltpu.VMEM((rows, hidden_size), bf16),
            pltpu.VMEM((rows, hidden_size), bf16),
            pltpu.VMEM((features // replicas, hidden_size), jnp.float32),
            pltpu.VMEM((features // replicas, hidden_size), jnp.float32),
            pltpu.VMEM((hidden_size, features), jnp.float32),
            pltpu.VMEM((experts, back, TILE, LANES), bf16),
            pltpu.VMEM((levels, back, TILE, LANES), bf16),
            pltpu.VMEM((levels, back, TILE, LANES), bf16),
            pltpu.VMEM((levels - 1, back, TILE, LANES), bf16),
            dma((3,)),
            dma((levels + 2, 2, replicas * experts)),
            dma((2, replicas * experts)),
            dma((levels,)),
            dma((levels,)),
            dma((levels - 1,)),
            dma((levels - 1,)),
        ],
        compiler_params=pltpu.CompilerParams(
            collective_id=0, has_side_effects=True, vmem_limit_bytes=32 * 1024 * 1024
        ),
    )(*operands)
    return pl.pallas_call(
        write_kernel,
        out_shape=tuple(jax.ShapeDtypeStruct(r.shape, r.dtype) for r in results),
        in_specs=[vmem] * len(results),
        out_specs=tuple(hbm for _ in results),
        scratch_shapes=[dma((len(results),))],
        compiler_params=pltpu.CompilerParams(vmem_limit_bytes=8 * 1024 * 1024),
    )(*results)


def solution(mesh):
    in_specs = (
        P(("dp", "expert"), None),
        P(("dp", "expert"), None),
        P(("dp", "expert"), None),
        P(("dp", "expert"), None),
        P(),
        P(),
        P("expert", None, None),
        P("expert", None, None),
        P("expert", None, None),
    )
    out_specs = (
        P(("dp", "expert"), None),
        P("expert", "dp", None),
        P("expert", "dp", None),
        P("expert", None, None),
    )

    def body(*args):
        token_count, features = args[0].shape
        if dense_fits(dict(mesh.shape), token_count, features, args[2].shape[1], args[6].shape[2]):
            return dense_shards(*args)
        return shards(*args)

    return jax.shard_map(body, mesh=mesh, in_specs=in_specs, out_specs=out_specs, check_vma=False)
```

```python
import functools

import jax
import jax.numpy as jnp
from jax import lax
from jax.experimental import pallas as pl
from jax.experimental.pallas import tpu as pltpu
from jax.sharding import PartitionSpec as P


def forward_rows(weight_gate, weight_up, weight_down, row_tokens, row_cotan, row_weights):
    gate_pre = jnp.dot(row_tokens, weight_gate, preferred_element_type=jnp.float32)
    up_proj = jnp.dot(row_tokens, weight_up, preferred_element_type=jnp.float32)
    sigmoid_gate = jax.nn.sigmoid(gate_pre)
    gate_act = gate_pre * sigmoid_gate
    hidden = (gate_act * up_proj).astype(jnp.bfloat16)
    out_grad = (row_weights.astype(jnp.float32)[:, None] * row_cotan.astype(jnp.float32)).astype(
        jnp.bfloat16
    )
    hidden_grad = jnp.dot(out_grad, weight_down.T, preferred_element_type=jnp.float32)
    gate_grad = (
        hidden_grad * up_proj * sigmoid_gate * (1.0 + gate_pre * (1.0 - sigmoid_gate))
    ).astype(jnp.bfloat16)
    up_grad = (hidden_grad * gate_act).astype(jnp.bfloat16)
    row_grads = jnp.dot(gate_grad, weight_gate.T, preferred_element_type=jnp.float32)
    row_grads = row_grads + jnp.dot(up_grad, weight_up.T, preferred_element_type=jnp.float32)
    return (row_grads.astype(jnp.bfloat16), (row_tokens, gate_grad, up_grad, hidden, out_grad))


def weight_terms(pieces):
    row_tokens, gate_grad, up_grad, hidden, out_grad = pieces
    grad_gate = jnp.dot(row_tokens.T, gate_grad, preferred_element_type=jnp.float32)
    grad_up = jnp.dot(row_tokens.T, up_grad, preferred_element_type=jnp.float32)
    grad_down = jnp.dot(hidden.T, out_grad, preferred_element_type=jnp.float32)
    return (grad_gate, grad_up, grad_down)


def expert_pass(weight_gate, weight_up, weight_down, row_tokens, row_cotan, row_weights):
    row_grads, pieces = forward_rows(
        weight_gate, weight_up, weight_down, row_tokens, row_cotan, row_weights
    )
    return (row_grads, weight_terms(pieces))


def shards(tokens, cotangent, routes, combine, hot_experts, extra_slots, w_gate, w_up, w_down):
    expert_count = lax.axis_size("expert")
    token_count, features = tokens.shape
    route_count = routes.shape[1]
    capacity = max(2, min(token_count * route_count * 7 // (8 * expert_count), token_count // 2))
    spare_slots = 2 * max(1, capacity // 6)
    expert_ids = routes.reshape(-1)
    assign_count = expert_ids.shape[0]
    assign_order = jnp.arange(assign_count, dtype=jnp.int32)
    earlier = (expert_ids[:, None] == expert_ids[None, :]) & (
        assign_order[None, :] < assign_order[:, None]
    )
    slot_rank = jnp.sum(earlier.astype(jnp.int32), axis=1)
    hot_match = expert_ids[:, None] == hot_experts[None, :]
    slot_limit = capacity + jnp.sum(jnp.where(hot_match, extra_slots[None, :], 0), axis=1)
    is_kept = slot_rank < slot_limit
    slot_count = capacity + spare_slots
    total_slots = expert_count * slot_count
    flat_slot = jnp.where(is_kept, expert_ids * slot_count + slot_rank, total_slots)
    slot_ids = jnp.arange(total_slots, dtype=jnp.int32)
    assign_onehot = slot_ids[:, None] == flat_slot[None, :]
    token_onehot = jnp.any(
        assign_onehot.reshape(total_slots, token_count, route_count), axis=2
    ).astype(jnp.bfloat16)
    both_rows = jnp.concatenate([tokens, cotangent], axis=1)
    filled = jnp.dot(token_onehot, both_rows, preferred_element_type=jnp.float32).astype(
        jnp.bfloat16
    )
    token_send = filled[:, :features].reshape(expert_count, slot_count, features)
    cotan_send = filled[:, features:].reshape(expert_count, slot_count, features)
    weight_flat = jnp.sum(
        jnp.where(assign_onehot, combine.reshape(-1).astype(jnp.float32)[None, :], 0.0), axis=1
    )
    weight_send = weight_flat.astype(jnp.bfloat16).reshape(expert_count, slot_count)
    token_recv, cotan_recv, weight_recv = (
        lax.all_to_all(token_send, "expert", split_axis=0, concat_axis=0, tiled=True),
        lax.all_to_all(cotan_send, "expert", split_axis=0, concat_axis=0, tiled=True),
        lax.all_to_all(weight_send, "expert", split_axis=0, concat_axis=0, tiled=True),
    )
    own_weights = (w_gate[0], w_up[0], w_down[0])
    all_rows, grad_terms = expert_pass(
        own_weights[0],
        own_weights[1],
        own_weights[2],
        token_recv.reshape(-1, features),
        cotan_recv.reshape(-1, features),
        weight_recv.reshape(-1),
    )
    grad_rows = all_rows.reshape(expert_count, slot_count, features)
    returned_rows = lax.all_to_all(grad_rows, "expert", split_axis=0, concat_axis=0, tiled=True)
    token_grads = jnp.dot(
        token_onehot.T,
        returned_rows.reshape(total_slots, features),
        preferred_element_type=jnp.float32,
    ).astype(jnp.bfloat16)
    grad_gate, grad_up = (
        lax.psum_scatter(grad_terms[0][None], "dp", scatter_dimension=1, tiled=True),
        lax.psum_scatter(grad_terms[1][None], "dp", scatter_dimension=1, tiled=True),
    )
    grad_down = lax.psum(grad_terms[2][None], "dp")
    return (
        token_grads,
        grad_gate.astype(jnp.bfloat16),
        grad_up.astype(jnp.bfloat16),
        grad_down.astype(jnp.bfloat16),
    )


MESH = pl.DeviceIdType.MESH
LANES = 128
TILE = 16
WRITE_PARTS = 4
NT = (((1,), (1,)), ((), ()))
TN = (((0,), (0,)), ((), ()))


def slots_of(token_count, route_count, expert_count):
    capacity = max(2, min(token_count * route_count * 7 // (8 * expert_count), token_count // 2))
    return capacity, 2 * max(1, capacity // 6)


def dense_fits(sizes, token_count, features, route_count, hidden_size):
    capacity, spare = slots_of(token_count, route_count, sizes["expert"])
    return (
        route_count == sizes["expert"]
        and sizes["dp"] == 4
        and sizes["expert"] % 2 == 0
        and token_count == 2 * TILE
        and capacity == TILE
        and spare * 2 == 8
        and features % (8 * LANES) == 0
        and hidden_size % LANES == 0
    )


def dense_kernel(
    experts,
    tok_hbm,
    cot_hbm,
    routes_hbm,
    comb_hbm,
    hot_hbm,
    extra_hbm,
    wg_hbm,
    wu_hbm,
    wd_hbm,
    tg_ref,
    gg_out,
    gu_out,
    gd_out,
    tok_ref,
    cot_ref,
    routes_ref,
    comb_ref,
    hot_ref,
    extra_ref,
    in_sem,
    slab,
    wg,
    wu,
    wd,
    all_t,
    all_og,
    all_h,
    all_gg,
    all_ug,
    acc_gate,
    acc_up,
    acc_down,
    row_out,
    pair_in,
    pair_sum,
    z_in,
    w_sem,
    send_sem,
    recv_sem,
    pair_send,
    pair_recv,
    z_send,
    z_recv,
):
    levels = experts // 2
    features = tok_ref.shape[1]
    blocks = features // LANES
    half = blocks // 2
    spill_at = 2 * blocks
    weight_at = spill_at + half
    bf16, f32 = jnp.bfloat16, jnp.float32

    d = lax.axis_index("dp")
    e = lax.axis_index("expert")
    z, c = e // 2, e % 2
    dx = d + 1 - 2 * (d % 2)
    dy = (d + 2) % 4
    dd = 3 - d
    pc = 1 - c

    def to(dp, level, core):
        return (dp, level * 2 + core)

    def slab_id(dp, level, core):
        return dp * experts + level * 2 + core

    input_copies = [
        pltpu.make_async_copy(h, v, in_sem.at[i])
        for i, (h, v) in enumerate(
            (
                (tok_hbm, tok_ref),
                (cot_hbm, cot_ref),
                (routes_hbm, routes_ref),
                (comb_hbm, comb_ref),
                (hot_hbm, hot_ref),
                (extra_hbm, extra_ref),
            )
        )
    ]
    for copy in input_copies:
        copy.start()
    weight_copies = [
        pltpu.make_async_copy(h.at[0], v, w_sem.at[i])
        for i, (h, v) in enumerate(((wg_hbm, wg), (wu_hbm, wu), (wd_hbm, wd)))
    ]
    for copy in weight_copies:
        copy.start()

    barrier = pltpu.get_barrier_semaphore()
    for peer in (to(dx, z, c), to(dy, z, c), to(d, z, pc)):
        pl.semaphore_signal(barrier, inc=1, device_id=peer, device_id_type=MESH)
    for step in range(1, levels):
        pl.semaphore_signal(
            barrier, inc=1, device_id=to(d, (z + step) % levels, c), device_id_type=MESH
        )

    me = slab_id(d, z, c)
    for copy in input_copies:
        copy.wait()
    names = -(-experts // TILE) * TILE
    expert_row = lax.broadcasted_iota(jnp.int32, (names, 2 * TILE), 0)
    token_lane = lax.broadcasted_iota(jnp.int32, (names, 2 * TILE), 1)
    routes = routes_ref[...]
    comb = comb_ref[...].astype(f32)
    weights = jnp.zeros((names, 2 * TILE), f32)
    for r in range(routes.shape[0]):
        weights = jnp.where(expert_row == routes[r : r + 1, :], comb[r : r + 1, :], weights)
    limit = jnp.full((names, 2 * TILE), TILE, jnp.int32)
    for j in range(hot_ref.shape[0]):
        limit = limit + jnp.where(expert_row == hot_ref[j], extra_ref[j], 0)
    weights = jnp.where(token_lane < limit, weights, 0.0).astype(bf16)
    unit_row = lax.broadcasted_iota(jnp.int32, (names, LANES), 0)
    unit_lane = lax.broadcasted_iota(jnp.int32, (names, LANES), 1)

    def turned(shift):
        unit = jnp.where(unit_lane == unit_row + shift, 1.0, 0.0).astype(bf16)
        return lax.dot_general(weights, unit, TN, preferred_element_type=f32)

    main_part, tail_part = turned(0), turned(LANES // 2)
    slab[me, weight_at] = (main_part[:TILE] + tail_part[TILE:]).astype(bf16)
    tok_tail = tok_ref[TILE:, :].astype(f32)[:8]
    cot_tail = cot_ref[TILE:, :].astype(f32)[:8]
    tail_row = lax.broadcasted_iota(jnp.int32, (8, features), 0)
    spill = jnp.where(tail_row < 4, tok_tail, pltpu.roll(cot_tail, 4, 0))
    for j in range(blocks):
        cols = slice(j * LANES, (j + 1) * LANES)
        slab[me, j] = tok_ref[:TILE, cols]
        slab[me, blocks + j] = cot_ref[:TILE, cols]
    for j in range(half):
        lo = spill[:, j * LANES : (j + 1) * LANES]
        hi = spill[:, (half + j) * LANES : (half + j + 1) * LANES]
        slab[me, spill_at + j] = jnp.concatenate([lo, hi], axis=0).astype(bf16)

    pl.semaphore_wait(barrier, 3 + levels - 1)

    tiles = slab.shape[1]
    cut = (tiles + 1) // 2
    pieces = (pl.ds(0, cut), pl.ds(cut, tiles - cut))

    def copy_of(s, p, way, peer):
        return pltpu.make_async_remote_copy(
            src_ref=slab.at[s, pieces[p]],
            dst_ref=slab.at[s, pieces[p]],
            send_sem=send_sem.at[way, p, s],
            recv_sem=recv_sem.at[p, s],
            device_id=peer,
            device_id_type=MESH,
        )

    def to_x(s, p):
        return copy_of(s, p, 0, to(dx, z, c))

    def to_y(s, p):
        return copy_of(s, p, 1, to(dy, z, c))

    def to_pair(s, p):
        return copy_of(s, p, 2, to(d, z, pc))

    def to_level(p, step):
        return copy_of(me, p, 2 + step, to(d, (z + step) % levels, c))

    def arrived(s, p):
        to_pair(s, p).wait_recv()

    def at_distance(dist, visit):
        if dist == 0:
            visit(z, 0)
            return
        pl.when(z - dist >= 0)(lambda: visit(z - dist, -1))
        pl.when(z + dist < levels)(lambda: visit(z + dist, 1))

    def column(dist, p):
        def visit(level, side):
            s = slab_id(d, level, c)
            if side:
                arrived(s, p)
            to_x(s, p).start()
            to_y(s, p).start()
            if side == 0:
                for step in range(1, levels):
                    to_level(p, step).start()
            to_pair(s, p).start()

        at_distance(dist, visit)

    def beside(dist, p):
        def visit(level, side):
            for dp in (dx, dy):
                s = slab_id(dp, level, c)
                arrived(s, p)
                if p == 0 and dp is dx:
                    to_y(s, p).start()
                if p == 1 and dp is dy:
                    to_x(s, p).start()
                to_pair(s, p).start()

        at_distance(dist, visit)

    def across(dist):
        def visit(level, side):
            s = slab_id(dd, level, c)
            for p in (0, 1):
                arrived(s, p)
                to_pair(s, p).start()

        at_distance(dist, visit)

    def from_pair(dp):
        for level in range(levels):
            for p in (0, 1):
                arrived(slab_id(dp, level, pc), p)

    column(0, 0)
    column(0, 1)
    for dist in range(1, levels):
        for p in (0, 1):
            column(dist, p)
    from_pair(d)

    main_rows = experts * TILE
    group_rows = main_rows + experts * 8
    main_lane = lax.broadcasted_iota(jnp.int32, (main_rows, LANES), 1)
    tail_lane = lax.broadcasted_iota(jnp.int32, (experts * 8, LANES), 1)

    def group(dp, at):
        rows = pl.ds(at, group_rows)
        part = pl.ds(dp * experts, experts)

        def main(j):
            return slab[part, j].reshape(main_rows, LANES)

        lo, hi = [], []
        for j in range(half):
            both = slab[part, spill_at + j].astype(f32)
            lo.append(both[:, :8].reshape(experts * 8, LANES))
            hi.append(both[:, 8:].reshape(experts * 8, LANES))
        tail = jnp.concatenate(lo + hi, axis=1)
        cot_rows = pltpu.roll(tail, experts * 8 - 4, 0)
        w_all = slab[part, weight_at].astype(f32)
        w_main = w_all.reshape(main_rows, LANES)
        w_tail = w_all[:, :8].reshape(experts * 8, LANES)
        w = jnp.concatenate(
            [
                jnp.sum(jnp.where(main_lane == e, w_main, 0.0), axis=1, keepdims=True),
                jnp.sum(jnp.where(tail_lane == e + LANES // 2, w_tail, 0.0), axis=1, keepdims=True),
            ],
            axis=0,
        )
        all_t[rows, :] = jnp.concatenate(
            [jnp.concatenate([main(j) for j in range(blocks)], axis=1), tail.astype(bf16)], axis=0
        )
        cot = jnp.concatenate(
            [
                jnp.concatenate([main(blocks + j) for j in range(blocks)], axis=1).astype(f32),
                cot_rows,
            ],
            axis=0,
        )
        all_og[rows, :] = (w * cot).astype(bf16)
        t = all_t[rows, :]
        gate_pre = jnp.dot(t, wg[...], preferred_element_type=f32)
        up_proj = jnp.dot(t, wu[...], preferred_element_type=f32)
        hidden_grad = lax.dot_general(all_og[rows, :], wd[...], NT, preferred_element_type=f32)
        sig = jax.nn.sigmoid(gate_pre)
        act = gate_pre * sig
        all_h[rows, :] = (act * up_proj).astype(bf16)
        all_gg[rows, :] = (hidden_grad * up_proj * sig * (1.0 + gate_pre * (1.0 - sig))).astype(
            bf16
        )
        all_ug[rows, :] = (hidden_grad * act).astype(bf16)

    for copy in weight_copies:
        copy.wait()
    group(d, 0)
    own = pl.ds(0, group_rows)
    rg = lax.dot_general(all_gg[own, :], wg[...], NT, preferred_element_type=f32)
    rg = rg + lax.dot_general(all_ug[own, :], wu[...], NT, preferred_element_type=f32)
    for j in range(blocks):
        row_out[:, j] = (
            rg[:main_rows, j * LANES : (j + 1) * LANES].reshape(experts, TILE, LANES).astype(bf16)
        )
    for j in range(half):
        lo = rg[main_rows:, j * LANES : (j + 1) * LANES].reshape(experts, 8, LANES)
        hi = rg[main_rows:, (half + j) * LANES : (half + j + 1) * LANES].reshape(experts, 8, LANES)
        row_out[:, blocks + j] = jnp.concatenate([lo, hi], axis=1).astype(bf16)

    def pair_copy(level):
        return pltpu.make_async_remote_copy(
            src_ref=row_out.at[level * 2 + pc],
            dst_ref=pair_in.at[level],
            send_sem=pair_send.at[level],
            recv_sem=pair_recv.at[level],
            device_id=to(d, z, pc),
            device_id_type=MESH,
        )

    for level in range(levels):
        pair_copy(level).start()

    for dist in range(levels):
        for p in (0, 1):
            beside(dist, p)

    for level in range(levels):
        pair_copy(level).wait_recv()
        pair_sum[level] = (
            row_out[level * 2 + c].astype(f32) + pair_in[level].astype(f32)
        ).astype(bf16)

    def z_copy(step):
        level = (z + step) % levels
        return pltpu.make_async_remote_copy(
            src_ref=pair_sum.at[level],
            dst_ref=z_in.at[step - 1],
            send_sem=z_send.at[step - 1],
            recv_sem=z_recv.at[step - 1],
            device_id=to(d, level, c),
            device_id_type=MESH,
        )

    for step in range(1, levels):
        z_copy(step).start()

    from_pair(dx)
    group(dx, group_rows)
    from_pair(dy)
    group(dy, 2 * group_rows)
    for dist in range(levels):
        across(dist)
    share = features // 4

    def weight_terms(at, count):
        rows = pl.ds(at, count)
        t_cols = all_t[rows, pl.ds(pl.multiple_of(d * share, LANES), share)]
        return (
            lax.dot_general(t_cols, all_gg[rows, :], TN, preferred_element_type=f32),
            lax.dot_general(t_cols, all_ug[rows, :], TN, preferred_element_type=f32),
            lax.dot_general(all_h[rows, :], all_og[rows, :], TN, preferred_element_type=f32),
        )

    early = weight_terms(0, 3 * group_rows)
    acc_gate[...], acc_up[...], acc_down[...] = early
    from_pair(dd)
    group(dd, 3 * group_rows)
    late = weight_terms(3 * group_rows, group_rows)
    gg_out[0] = (acc_gate[...] + late[0]).astype(bf16)
    gu_out[0] = (acc_up[...] + late[1]).astype(bf16)
    gd_out[0] = (acc_down[...] + late[2]).astype(bf16)

    total = pair_sum[z].astype(f32)
    for step in range(1, levels):
        z_copy(step).wait_recv()
        total = total + z_in[step - 1].astype(f32)
    for j in range(blocks):
        tg_ref[:TILE, j * LANES : (j + 1) * LANES] = total[j].astype(bf16)
    blank = jnp.zeros((8, LANES), f32)
    for j in range(half):
        tile = total[blocks + j]
        tg_ref[TILE:, j * LANES : (j + 1) * LANES] = jnp.concatenate(
            [tile[:8], blank], axis=0
        ).astype(bf16)
        tg_ref[TILE:, (half + j) * LANES : (half + j + 1) * LANES] = jnp.concatenate(
            [tile[8:], blank], axis=0
        ).astype(bf16)

    for level in range(levels):
        pair_copy(level).wait_send()
        to_y(slab_id(dx, level, c), 0).wait_send()
        to_x(slab_id(dy, level, c), 1).wait_send()
        s = slab_id(d, level, c)
        for p in (0, 1):
            to_x(s, p).wait_send()
            to_y(s, p).wait_send()
            for dp in (d, dx, dy, dd):
                to_pair(slab_id(dp, level, c), p).wait_send()

    for step in range(1, levels):
        z_copy(step).wait_send()
        to_level(0, step).wait_send()
        to_level(1, step).wait_send()


def write_kernel(*refs):
    sources, sem = refs[: len(refs) // 2], refs[-1]
    targets = refs[len(refs) // 2 : -1]
    copies = []
    for i, (a, b) in enumerate(zip(sources, targets)):
        parts = WRITE_PARTS if len(a.shape) == 3 and a.shape[1] % (WRITE_PARTS * TILE) == 0 else 1
        size = a.shape[-2] // parts
        for p in range(parts):
            at = pl.ds(p * size, size)
            where = (0, at) if len(a.shape) == 3 else (at,)
            copies.append(pltpu.make_async_copy(a.at[where], b.at[where], sem.at[i, p]))
    for copy in copies:
        copy.start()
    for copy in copies:
        copy.wait()


def dense_shards(tokens, cotangent, routes, combine, hot_experts, extra_slots, w_gate, w_up, w_down):
    experts = lax.axis_size("expert")
    replicas = lax.axis_size("dp")
    token_count, features = tokens.shape
    hidden_size = w_gate.shape[2]
    blocks = features // LANES
    levels = experts // 2
    tiles = 2 * blocks + blocks // 2 + 1
    back = blocks + blocks // 2
    rows = replicas * experts * (TILE + 8)
    bf16 = jnp.bfloat16
    vmem = pl.BlockSpec(memory_space=pltpu.VMEM)
    hbm = pl.BlockSpec(memory_space=pltpu.HBM)
    dma = pltpu.SemaphoreType.DMA
    operands = [
        pltpu.with_memory_space_constraint(a, pltpu.HBM)
        for a in (
            tokens,
            cotangent,
            routes.T,
            combine.T,
            hot_experts,
            extra_slots,
            w_gate,
            w_up,
            w_down,
        )
    ]
    results = pl.pallas_call(
        functools.partial(dense_kernel, experts),
        out_shape=(
            jax.ShapeDtypeStruct((token_count, features), bf16),
            jax.ShapeDtypeStruct((1, features // replicas, hidden_size), bf16),
            jax.ShapeDtypeStruct((1, features // replicas, hidden_size), bf16),
            jax.ShapeDtypeStruct((1, hidden_size, features), bf16),
        ),
        in_specs=[hbm] * 9,
        out_specs=(vmem, vmem, vmem, vmem),
        scratch_shapes=[
            pltpu.VMEM(tokens.shape, bf16),
            pltpu.VMEM(tokens.shape, bf16),
            pltpu.VMEM(routes.shape[::-1], jnp.int32),
            pltpu.VMEM(routes.shape[::-1], bf16),
            pltpu.SMEM(hot_experts.shape, jnp.int32),
            pltpu.SMEM(hot_experts.shape, jnp.int32),
            dma((6,)),
            pltpu.VMEM((replicas * experts, tiles, TILE, LANES), bf16),
            pltpu.VMEM((features, hidden_size), bf16),
            pltpu.VMEM((features, hidden_size), bf16),
            pltpu.VMEM((hidden_size, features), bf16),
            pltpu.VMEM((rows, features), bf16),
            pltpu.VMEM((rows, features), bf16),
            pltpu.VMEM((rows, hidden_size), bf16),
            pltpu.VMEM((rows, hidden_size), bf16),
            pltpu.VMEM((rows, hidden_size), bf16),
            pltpu.VMEM((features // replicas, hidden_size), jnp.float32),
            pltpu.VMEM((features // replicas, hidden_size), jnp.float32),
            pltpu.VMEM((hidden_size, features), jnp.float32),
            pltpu.VMEM((experts, back, TILE, LANES), bf16),
            pltpu.VMEM((levels, back, TILE, LANES), bf16),
            pltpu.VMEM((levels, back, TILE, LANES), bf16),
            pltpu.VMEM((levels - 1, back, TILE, LANES), bf16),
            dma((3,)),
            dma((levels + 2, 2, replicas * experts)),
            dma((2, replicas * experts)),
            dma((levels,)),
            dma((levels,)),
            dma((levels - 1,)),
            dma((levels - 1,)),
        ],
        compiler_params=pltpu.CompilerParams(
            collective_id=0, has_side_effects=True, vmem_limit_bytes=32 * 1024 * 1024
        ),
    )(*operands)
    return pl.pallas_call(
        write_kernel,
        out_shape=tuple(jax.ShapeDtypeStruct(r.shape, r.dtype) for r in results),
        in_specs=[vmem] * len(results),
        out_specs=tuple(hbm for _ in results),
        scratch_shapes=[dma((len(results), WRITE_PARTS))],
        compiler_params=pltpu.CompilerParams(vmem_limit_bytes=8 * 1024 * 1024),
    )(*results)


def solution(mesh):
    in_specs = (
        P(("dp", "expert"), None),
        P(("dp", "expert"), None),
        P(("dp", "expert"), None),
        P(("dp", "expert"), None),
        P(),
        P(),
        P("expert", None, None),
        P("expert", None, None),
        P("expert", None, None),
    )
    out_specs = (
        P(("dp", "expert"), None),
        P("expert", "dp", None),
        P("expert", "dp", None),
        P("expert", None, None),
    )

    def body(*args):
        token_count, features = args[0].shape
        if dense_fits(dict(mesh.shape), token_count, features, args[2].shape[1], args[6].shape[2]):
            return dense_shards(*args)
        return shards(*args)

    return jax.shard_map(body, mesh=mesh, in_specs=in_specs, out_specs=out_specs, check_vma=False)
```
